32 devices in a mesh: parts: 2 (over y), pencil: 4 (over z), slab: 2 (over x), field: 2 (over core).
Axes of the slice: x: 2, y: 2, z: 4, core: 2. Of those that a mesh axis runs over, the one named last changes fastest.
Arguments:
- state: bfloat16 [16, 2, 512, 512], P('parts', 'slab', 'pencil'), parts along dimension 0, may hold values from -6 to 6
- tangents: bfloat16 [16, 8, 2, 512, 512], P(('parts', 'field'), None, 'slab', 'pencil'), parts along dimension 0, may hold values from -6 to 6
- d1: bfloat16 [512, 512], replicated, may hold values from -0.25 to 0.25
- d2: bfloat16 [512, 512], replicated, may hold values from -0.25 to 0.25
- filt: bfloat16 [512, 512], replicated, may hold values from -0.25 to 0.25
- advect: float32 [2, 8], replicated, may hold values from 0.3 to 1
- diffuse: float32 [8], replicated, may hold values from 0.3 to 1
- coef: float32 [8, 8], replicated, may hold values from -3 to 3
- rates: float32 [8, 8], replicated, may hold values from -3.6 to 3.6
Outputs:
- state_out: bfloat16 [16, 2, 512, 512], P('parts', 'slab', 'pencil'), parts along dimension 0
- tangent_out: bfloat16 [16, 8, 2, 512, 512], P(('parts', 'field'), None, 'slab', 'pencil'), parts along dimension 0
The draws below stay inside these ranges and needn't reach their ends.
There are 2 independent parts, one for each index of `parts`. The reference program is written for one: setup_inputs(seed, part) draws one part's arguments, and reference() takes and returns one part's arrays. A program takes and returns all parts, laid end to end along the dimension named above; an argument that names none is the same for every part. Nothing has to cross between parts.
All inputs are finite; a program needn't handle non-finite values.
Results may differ from the reference program's by a relative error of at most 0.0094.
Values may be sent and summed in bfloat16 or wider, within the bound.
No kernel may reach another device: no remote copies, remote signals or barrier semaphores. Data moves between devices by JAX's collectives and lax.ppermute only.
A program may use at most 128 MiB of HBM per device.

```python
import jax
import jax.numpy as jnp
from jax import lax

N = 512
S = 8
K = 8
STEPS = 1
NZ = 2


def steps_of(key, dims, cuts, low, high):
    factor_of = 1.0
    for dim, blocks in cuts:
        draws = jax.random.uniform(jax.random.fold_in(jax.random.fold_in(key, 6), dim), (blocks,), jnp.float32, low / len(cuts), high / len(cuts))
        factor_of = factor_of * jnp.repeat(jnp.exp(draws), dims[dim] // blocks).reshape((-1,) + (1,) * (len(dims) - 1 - dim))
    return factor_of


def scatter_about(key, extent, width, most, cuts=(), kind=jnp.bfloat16):
    array = width * jax.random.normal(key, extent, jnp.float32)
    if cuts:
        array = array * steps_of(key, extent, cuts, -0.22, 0.18)
    return jnp.clip(array, -most, most).astype(kind)


def setup_inputs(seed: int = 0, part: int = 0) -> dict:
    keys = jax.random.split(jax.random.key(seed), 10)
    own_keys = jax.random.split(jax.random.fold_in(keys[9], part), 10)
    state = scatter_about(own_keys[0], (S, NZ, N, N), 1.0, 6.0, ((1, 2), (2, 4)))
    tangents = scatter_about(own_keys[1], (K, S, NZ, N, N), 1.0, 6.0, ((0, 2), (2, 2), (3, 4)))
    d1 = scatter_about(keys[2], (N, N), N ** -0.5, 0.25)
    d2 = scatter_about(keys[3], (N, N), N ** -0.5, 0.25)
    filt = scatter_about(keys[4], (N, N), N ** -0.5, 0.25)
    advect = jnp.clip(jax.random.uniform(keys[5], (2, S), jnp.float32, 0.3, 1.0), 0.3, 1.0)
    diffuse = jnp.clip(jax.random.uniform(keys[6], (S,), jnp.float32, 0.3, 1.0), 0.3, 1.0)
    coef = scatter_about(keys[7], (K, S), 0.5, 3.0, (), jnp.float32)
    rates = scatter_about(keys[8], (K, S), 0.6, 3.6, (), jnp.float32)
    return {"state": state, "tangents": tangents, "d1": d1, "d2": d2, "filt": filt, "advect": advect, "diffuse": diffuse, "coef": coef, "rates": rates}


highest = lax.Precision.HIGHEST
time_step = 0.4


def spread(values, fields):
    return values.reshape(values.shape + (1,) * (fields.ndim - values.ndim))


def reaction(state, tangent, coef, rates, offset):
    state_float = state.astype(jnp.float32)
    argument = jnp.einsum('ps,s...->p...', rates, state_float, precision=highest)
    activity = jnp.tanh(argument)
    slopes = 1.0 - activity * activity
    state_rate = jnp.einsum('ps,p...->s...', coef, activity, precision=highest)
    tangent_float = tangent.astype(jnp.float32)
    mixing = jnp.einsum('pt,qt...->qp...', rates, tangent_float, precision=highest)
    number = tangent.shape[0]
    own_coef = lax.dynamic_slice_in_dim(coef, offset, number, 0)
    own_activity = lax.dynamic_slice_in_dim(activity, offset, number, 0)
    tangent_rate = jnp.einsum('ps,qp...->qs...', coef, slopes[None] * mixing, precision=highest)
    tangent_rate = tangent_rate + spread(own_coef, tangent) * own_activity[:, None]
    return state_rate, tangent_rate


def update(fields, rate, speeds, diffusivity, operators):
    derivative_op, diffusion_op, filter_op = operators
    slope_term = jnp.dot(fields, derivative_op, preferred_element_type=jnp.float32)
    curve_term = jnp.dot(fields, diffusion_op, preferred_element_type=jnp.float32)
    middle = fields.astype(jnp.float32) + time_step * (
        spread(diffusivity, fields) * curve_term - spread(speeds, fields) * slope_term + rate)
    middle = middle.astype(jnp.bfloat16)
    return jnp.dot(middle, filter_op, preferred_element_type=jnp.float32).astype(jnp.bfloat16)


def reference(state, tangents, d1, d2, filt, advect, diffuse, coef, rates):
    operators = (d1, d2, filt)

    def plane(pair):
        plane_state, plane_tangent = pair
        for section in range(STEPS):
            for direction in range(2):
                speeds = advect[direction]
                state_rate, tangent_rate = reaction(plane_state, plane_tangent, coef, rates, 0)
                plane_tangent = update(plane_tangent, tangent_rate, speeds[None, :], diffuse[None, :], operators)
                plane_state = update(plane_state, state_rate, speeds, diffuse, operators)
                plane_state = jnp.swapaxes(plane_state, -1, -2)
                plane_tangent = jnp.swapaxes(plane_tangent, -1, -2)
        return plane_state, plane_tangent

    result_state, result_tangent = lax.map(plane, (jnp.moveaxis(state, 1, 0), jnp.moveaxis(tangents, 2, 0)))
    return jnp.moveaxis(result_state, 0, 1), jnp.moveaxis(result_tangent, 0, 2)
```

```python
import functools

import jax
import jax.numpy as jnp
from jax import lax
from jax.experimental import pallas as pl
from jax.experimental.pallas import tpu as pltpu
from jax.sharding import PartitionSpec as P


highest = lax.Precision.HIGHEST
time_step = 0.4
f32 = jnp.float32
bf16 = jnp.bfloat16
LANES = 128
TILE = 16


def spread(values, fields):
    return values.reshape(values.shape + (1,) * (fields.ndim - values.ndim))


def reaction(state, tangent, coef, rates, offset):
    state_float = state.astype(f32)
    argument = jnp.einsum("ps,s...->p...", rates, state_float, precision=highest)
    activity = jnp.tanh(argument)
    slopes = 1.0 - activity * activity
    state_rate = jnp.einsum("ps,p...->s...", coef, activity, precision=highest)
    tangent_float = tangent.astype(f32)
    mixing = jnp.einsum("pt,qt...->qp...", rates, tangent_float, precision=highest)
    number = tangent.shape[0]
    own_coef = lax.dynamic_slice_in_dim(coef, offset, number, 0)
    own_activity = lax.dynamic_slice_in_dim(activity, offset, number, 0)
    tangent_rate = jnp.einsum("ps,qp...->qs...", coef, slopes[None] * mixing, precision=highest)
    tangent_rate = tangent_rate + spread(own_coef, tangent) * own_activity[:, None]
    return (state_rate, tangent_rate)


def update(fields, rate, speeds, diffusivity, operators):
    derivative_op, diffusion_op, filter_op = operators
    slope_term = jnp.dot(fields, derivative_op, preferred_element_type=f32)
    curve_term = jnp.dot(fields, diffusion_op, preferred_element_type=f32)
    middle = fields.astype(f32) + time_step * (
        spread(diffusivity, fields) * curve_term - spread(speeds, fields) * slope_term + rate
    )
    middle = middle.astype(bf16)
    return jnp.dot(middle, filter_op, preferred_element_type=f32).astype(bf16)


def plain(state, tangents, d1, d2, filt, advect, diffuse, coef, rates):
    params_here = tangents.shape[0]
    state_count = state.shape[0]
    offset = lax.axis_index("field") * params_here
    operators = (d1, d2, filt)
    for direction in range(2):
        speeds = advect[direction]
        state_rate, tangent_rate = reaction(state, tangents, coef, rates, offset)
        tangents = update(tangents, tangent_rate, speeds[None, :], diffuse[None, :], operators)
        outgoing = update(state, state_rate, speeds, diffuse, operators)
        merged = tangents.reshape((params_here * state_count,) + tangents.shape[2:])
        arrived = lax.all_to_all(outgoing, "pencil", split_axis=3, concat_axis=2, tiled=True)
        merged = lax.all_to_all(merged, "pencil", split_axis=3, concat_axis=2, tiled=True)
        state = jnp.swapaxes(arrived, 2, 3)
        merged = jnp.swapaxes(merged, 2, 3)
        tangents = merged.reshape((params_here, state_count) + merged.shape[1:])
    return (state, tangents)


def weighted(weights, arrays):
    total = None
    for weight, array in zip(weights, arrays):
        term = weight * array
        total = term if total is None else total + term
    return total


def activities(rates, u):
    count = rates.shape[0]
    return [jnp.tanh(weighted([rates[p, t] for t in range(len(u))], u)) for p in range(count)]


def tangent_rates(rates, coef, u, w, own):
    acts = activities(rates, u)
    own_act = jnp.tanh(weighted([rates[own, t] for t in range(len(u))], u))
    scaled = []
    for p, act in enumerate(acts):
        mix = weighted([rates[p, t] for t in range(len(w))], w)
        scaled.append((1.0 - act * act) * mix)
    return [
        weighted([coef[p, s] for p in range(len(scaled))], scaled) + coef[own, s] * own_act
        for s in range(len(w))
    ]


def advance(v, curve, slope, rate, diffusivity, speed):
    return (v + time_step * (diffusivity * curve - speed * slope + rate)).astype(bf16)


def aligned(index, size):
    return pl.ds(pl.multiple_of(index * size, size), size)


def permute_filter(filt, filt_own, me, n):
    size = filt.shape[1] // n

    @pl.when(pl.program_id(0) == 0)
    def _():
        for r in range(n):
            filt_own[:, r * size : (r + 1) * size] = filt[:, aligned(me ^ r, size)]


def x_state_kernel(n, rates, coef, advect, diffuse, state, d1, d2, filt, *rest):
    outs, (filt_own, slope, curve, middle) = rest[:n], rest[n:]
    me, half = lax.axis_index("pencil"), lax.axis_index("field")
    count, rows, length = state.shape
    here = outs[0].shape[0]
    first = half * here
    size = length // n
    permute_filter(filt, filt_own, me, n)
    own = state[pl.ds(first, here)].reshape(here * rows, length)
    slope[...] = jnp.dot(own, d1[...], preferred_element_type=f32)
    curve[...] = jnp.dot(own, d2[...], preferred_element_type=f32)

    def tile(i, carry):
        down = pl.ds(pl.multiple_of(i * TILE, TILE), TILE)
        for c in range(length // LANES):
            across = slice(c * LANES, (c + 1) * LANES)
            u = [state[t, down, across].astype(f32) for t in range(count)]
            acts = activities(rates, u)
            for s in range(here):
                at = pl.ds(pl.multiple_of(s * rows + i * TILE, TILE), TILE)
                rate = weighted([coef[p, first + s] for p in range(len(acts))], acts)
                v = state[first + s, down, across].astype(f32)
                middle[at, across] = advance(
                    v, curve[at, across], slope[at, across], rate, diffuse[first + s], advect[0, first + s]
                )
        return carry

    lax.fori_loop(0, rows // TILE, tile, 0)
    result = jnp.dot(middle[...], filt_own[...], preferred_element_type=f32).astype(bf16)
    for r in range(n):
        outs[r][...] = result[:, r * size : (r + 1) * size].reshape(here, rows, size)


def x_tangent_kernel(n, q, params_here, rates, coef, advect, diffuse, state, tangent, d1, d2, filt, *rest):
    outs, (filt_own, slope, curve, middle) = rest[:n], rest[n:]
    me, half = lax.axis_index("pencil"), lax.axis_index("field")
    count, rows, length = state.shape
    size = length // n
    permute_filter(filt, filt_own, me, n)
    own = tangent[...].reshape(count * rows, length)
    slope[...] = jnp.dot(own, d1[...], preferred_element_type=f32)
    curve[...] = jnp.dot(own, d2[...], preferred_element_type=f32)

    def tile(i, carry):
        down = pl.ds(pl.multiple_of(i * TILE, TILE), TILE)
        for c in range(length // LANES):
            across = slice(c * LANES, (c + 1) * LANES)
            u = [state[t, down, across].astype(f32) for t in range(count)]
            w = [tangent[t, down, across].astype(f32) for t in range(count)]
            rate = tangent_rates(rates, coef, u, w, half * params_here + q)
            for s in range(count):
                at = pl.ds(pl.multiple_of(s * rows + i * TILE, TILE), TILE)
                middle[at, across] = advance(
                    w[s], curve[at, across], slope[at, across], rate[s], diffuse[s], advect[0, s]
                )
        return carry

    lax.fori_loop(0, rows // TILE, tile, 0)
    result = jnp.dot(middle[...], filt_own[...], preferred_element_type=f32).astype(bf16)
    for r in range(n):
        outs[r][...] = result[:, r * size : (r + 1) * size].reshape(count, rows, size)


def gather_slots(slots, full, me, first):
    for r, slot in enumerate(slots):
        down = aligned(me ^ r, slot.shape[1])
        for s in range(slot.shape[0]):
            full[down, aligned(first + s, LANES)] = slot[s]


def y_kernel(n, q, params_here, rates, coef, advect, diffuse, *rest):
    own, rest = rest[:n], rest[n:]
    other, rest = rest[:n], rest[n:]
    if q is not None:
        arrived, rest = rest[:n], rest[n:]
    d1t, d2t, filtt = rest[:3]
    outs, rest = rest[3 : 3 + n], rest[3 + n :]
    u_full, v_full, middle, slope, curve = rest
    me, half = lax.axis_index("pencil"), lax.axis_index("field")
    here = own[0].shape[0]
    count = rates.shape[1]
    length = d1t.shape[0]
    size = length // n
    fields = outs[0].shape[0]
    step = slope.shape[0]
    gather_slots(own, u_full, me, half * here)
    gather_slots(other, u_full, me, (1 - half) * here)
    if q is None:
        first = half * here
        for r, slot in enumerate(own):
            for s in range(here):
                v_full[aligned(me ^ r, size), s * LANES : (s + 1) * LANES] = slot[s]
    else:
        first = 0
        for r, slot in enumerate(arrived):
            for s in range(count):
                v_full[aligned(me ^ r, size), s * LANES : (s + 1) * LANES] = slot[s]

    def block(b, carry):
        down = pl.ds(pl.multiple_of(b * step, step), step)
        slope[...] = jnp.dot(d1t[down, :], v_full[...], preferred_element_type=f32)
        curve[...] = jnp.dot(d2t[down, :], v_full[...], preferred_element_type=f32)

        def tile(i, inner):
            at = pl.ds(pl.multiple_of(i * TILE, TILE), TILE)
            row = pl.ds(pl.multiple_of(b * step + i * TILE, TILE), TILE)
            u = [u_full[row, t * LANES : (t + 1) * LANES].astype(f32) for t in range(count)]
            v = [v_full[row, s * LANES : (s + 1) * LANES].astype(f32) for s in range(fields)]
            if q is None:
                acts = activities(rates, u)
                rate = [
                    weighted([coef[p, first + s] for p in range(len(acts))], acts) for s in range(fields)
                ]
            else:
                rate = tangent_rates(rates, coef, u, v, half * params_here + q)
            for s in range(fields):
                across = slice(s * LANES, (s + 1) * LANES)
                middle[row, across] = advance(
                    v[s], curve[at, across], slope[at, across], rate[s], diffuse[first + s], advect[1, first + s]
                )
            return inner

        lax.fori_loop(0, step // TILE, tile, 0)
        return carry

    lax.fori_loop(0, length // step, block, 0)
    for r in range(n):
        result = jnp.dot(filtt[aligned(me ^ r, size), :], middle[...], preferred_element_type=f32).astype(bf16)
        for s in range(fields):
            outs[r][s] = result[:, s * LANES : (s + 1) * LANES]


def place_kernel(n, slots_of, *rest):
    me, half = lax.axis_index("pencil"), lax.axis_index("field")
    out = rest[-1]
    slots = rest[: n * slots_of]
    here = slots[0].shape[0]
    size = slots[0].shape[2]
    for g in range(slots_of):
        for r in range(n):
            slot = slots[g * n + r]
            for s in range(here):
                if slots_of == 1:
                    out[0, s, 0, :, aligned(me ^ r, size)] = slot[s]
                else:
                    at = (half if g == 0 else 1 - half) * here + s
                    out[at, 0, :, aligned(me ^ r, size)] = slot[s]


SMEM = pl.BlockSpec(memory_space=pltpu.SMEM)
VMEM = pl.BlockSpec(memory_space=pltpu.VMEM)
HBM = pl.BlockSpec(memory_space=pl.ANY)
LIMIT = 48 * 1024 * 1024


def cost(flops, moved):
    return pl.CostEstimate(flops=flops, bytes_accessed=moved, transcendentals=0)


def x_call(n, q, scalars, state, tangents, d1, d2, filt, here):
    count, _, deep, length = state.shape
    rows = min(deep, 32)
    size = length // n
    fields = here if q is None else count
    whole = pl.BlockSpec((length, length), lambda i: (0, 0))
    arrays = [state]
    specs = [pl.BlockSpec((count, None, rows, length), lambda i: (0, 0, i, 0))]
    if q is None:
        body = functools.partial(x_state_kernel, n)
    else:
        body = functools.partial(x_tangent_kernel, n, q, tangents.shape[0])
        arrays.append(tangents)
        specs.append(pl.BlockSpec((None, count, None, rows, length), lambda i: (q, 0, 0, i, 0)))
    return pl.pallas_call(
        body,
        grid=(deep // rows,),
        out_shape=[jax.ShapeDtypeStruct((fields, deep, size), bf16)] * n,
        in_specs=[SMEM] * 4 + specs + [whole] * 3,
        out_specs=[pl.BlockSpec((fields, rows, size), lambda i: (0, i, 0))] * n,
        scratch_shapes=[
            pltpu.VMEM((length, length), bf16),
            pltpu.VMEM((fields * rows, length), f32),
            pltpu.VMEM((fields * rows, length), f32),
            pltpu.VMEM((fields * rows, length), bf16),
        ],
        compiler_params=pltpu.CompilerParams(vmem_limit_bytes=LIMIT),
        cost_estimate=cost(6 * fields * deep * length * length, 4 * fields * deep * length),
        name="x_state" if q is None else f"x_tangent{q}",
    )(*scalars, *arrays, d1, d2, filt)


def y_call(n, q, params_here, scalars, own, other, arrived, turned):
    here, deep, size = own[0].shape
    count = scalars[0].shape[1]
    length = deep * n
    fields = here if q is None else count
    step = min(length, 128)
    arrays = list(own) + list(other) + list(arrived or ())
    return pl.pallas_call(
        functools.partial(y_kernel, n, q, params_here),
        out_shape=[jax.ShapeDtypeStruct((fields, deep, size), bf16)] * n,
        in_specs=[SMEM] * 4 + [VMEM] * (len(arrays) + 3),
        out_specs=[VMEM] * n,
        scratch_shapes=[
            pltpu.VMEM((length, count * LANES), bf16),
            pltpu.VMEM((length, fields * LANES), bf16),
            pltpu.VMEM((length, fields * LANES), bf16),
            pltpu.VMEM((step, fields * LANES), f32),
            pltpu.VMEM((step, fields * LANES), f32),
        ],
        compiler_params=pltpu.CompilerParams(vmem_limit_bytes=LIMIT),
        cost_estimate=cost(6 * fields * deep * length * length, 4 * fields * deep * length),
        name="y_state" if q is None else f"y_tangent{q}",
    )(*scalars, *arrays, *turned)


def place_state(n, shape, own, other):
    return pl.pallas_call(
        functools.partial(place_kernel, n, 2),
        out_shape=jax.ShapeDtypeStruct(shape, bf16),
        in_specs=[VMEM] * (2 * n),
        out_specs=VMEM,
        compiler_params=pltpu.CompilerParams(vmem_limit_bytes=LIMIT),
        name="place_state",
    )(*own, *other)


def place_tangent(n, q, shape, slots, buffer):
    count, deep, size = slots[0].shape
    part = 2
    specs = [pl.BlockSpec((part, deep, size), lambda i: (i, 0, 0))] * n
    arrays = list(slots)
    aliases = {}
    if buffer is not None:
        specs.append(HBM)
        arrays.append(buffer)
        aliases = {n: 0}
    return pl.pallas_call(
        functools.partial(place_kernel, n, 1),
        grid=(count // part,),
        out_shape=jax.ShapeDtypeStruct(shape, bf16),
        in_specs=specs,
        out_specs=pl.BlockSpec((1, part, 1, deep, shape[-1]), lambda i: (q, i, 0, 0, 0)),
        input_output_aliases=aliases,
        compiler_params=pltpu.CompilerParams(vmem_limit_bytes=LIMIT),
        name=f"place_tangent{q}",
    )(*arrays)


def exchange(n, slots):
    return [slots[0]] + [
        lax.ppermute(slots[r], "pencil", [(i, i ^ r) for i in range(n)]) for r in range(1, n)
    ]


def swap(slots):
    return [lax.ppermute(slot, "field", [(0, 1), (1, 0)]) for slot in slots]


def pipelined(n, state, tangents, d1, d2, filt, advect, diffuse, coef, rates):
    params_here = tangents.shape[0]
    here = state.shape[0] // 2
    scalars = (rates, coef, advect, diffuse)
    own = exchange(n, x_call(n, None, scalars, state, None, d1, d2, filt, here))
    sent = [
        exchange(n, x_call(n, q, scalars, state, tangents, d1, d2, filt, here)) for q in range(params_here)
    ]
    turned = (d1.T, d2.T, filt.T)
    other = swap(own)
    mine = exchange(n, y_call(n, None, params_here, scalars, own, other, None, turned))
    buffer = None
    for q in range(params_here):
        back = exchange(n, y_call(n, q, params_here, scalars, own, other, sent[q], turned))
        buffer = place_tangent(n, q, tangents.shape, back, buffer)
    return (place_state(n, state.shape, mine, swap(mine)), buffer)


def solution(mesh):
    in_specs = (
        P("parts", "slab", "pencil", None),
        P(("parts", "field"), None, "slab", "pencil", None),
        P(),
        P(),
        P(),
        P(),
        P(),
        P(),
        P(),
    )
    out_specs = (
        P("parts", "slab", "pencil", None),
        P(("parts", "field"), None, "slab", "pencil", None),
    )
    n = mesh.shape["pencil"]

    def local(state, tangents, *others):
        count, planes, deep, length = state.shape
        fits = (
            n & (n - 1) == 0
            and mesh.shape["field"] == 2
            and count % 2 == 0
            and planes == 1
            and deep == LANES
            and deep * n == length
        )
        if fits:
            return pipelined(n, state, tangents, *others)
        return plain(state, tangents, *others)

    return jax.shard_map(local, mesh=mesh, in_specs=in_specs, out_specs=out_specs, check_vma=False)
```

```python
import functools

import jax
import jax.numpy as jnp
from jax import lax
from jax.experimental import pallas as pl
from jax.experimental.pallas import tpu as pltpu
from jax.sharding import PartitionSpec as P


highest = lax.Precision.HIGHEST
time_step = 0.4
f32 = jnp.float32
bf16 = jnp.bfloat16
LANES = 128
WIDE = 2 * LANES
DEPTH = 32


def spread(values, fields):
    return values.reshape(values.shape + (1,) * (fields.ndim - values.ndim))


def reaction(state, tangent, coef, rates, offset):
    state_float = state.astype(f32)
    argument = jnp.einsum("ps,s...->p...", rates, state_float, precision=highest)
    activity = jnp.tanh(argument)
    slopes = 1.0 - activity * activity
    state_rate = jnp.einsum("ps,p...->s...", coef, activity, precision=highest)
    tangent_float = tangent.astype(f32)
    mixing = jnp.einsum("pt,qt...->qp...", rates, tangent_float, precision=highest)
    number = tangent.shape[0]
    own_coef = lax.dynamic_slice_in_dim(coef, offset, number, 0)
    own_activity = lax.dynamic_slice_in_dim(activity, offset, number, 0)
    tangent_rate = jnp.einsum("ps,qp...->qs...", coef, slopes[None] * mixing, precision=highest)
    tangent_rate = tangent_rate + spread(own_coef, tangent) * own_activity[:, None]
    return (state_rate, tangent_rate)


def update(fields, rate, speeds, diffusivity, operators):
    derivative_op, diffusion_op, filter_op = operators
    slope_term = jnp.dot(fields, derivative_op, preferred_element_type=f32)
    curve_term = jnp.dot(fields, diffusion_op, preferred_element_type=f32)
    middle = fields.astype(f32) + time_step * (
        spread(diffusivity, fields) * curve_term - spread(speeds, fields) * slope_term + rate
    )
    middle = middle.astype(bf16)
    return jnp.dot(middle, filter_op, preferred_element_type=f32).astype(bf16)


def plain(state, tangents, d1, d2, filt, advect, diffuse, coef, rates):
    params_here = tangents.shape[0]
    state_count = state.shape[0]
    offset = lax.axis_index("field") * params_here
    operators = (d1, d2, filt)
    for direction in range(2):
        speeds = advect[direction]
        state_rate, tangent_rate = reaction(state, tangents, coef, rates, offset)
        tangents = update(tangents, tangent_rate, speeds[None, :], diffuse[None, :], operators)
        outgoing = update(state, state_rate, speeds, diffuse, operators)
        merged = tangents.reshape((params_here * state_count,) + tangents.shape[2:])
        arrived = lax.all_to_all(outgoing, "pencil", split_axis=3, concat_axis=2, tiled=True)
        merged = lax.all_to_all(merged, "pencil", split_axis=3, concat_axis=2, tiled=True)
        state = jnp.swapaxes(arrived, 2, 3)
        merged = jnp.swapaxes(merged, 2, 3)
        tangents = merged.reshape((params_here, state_count) + merged.shape[1:])
    return (state, tangents)


def aligned(index, size):
    return pl.ds(pl.multiple_of(index * size, size), size)


def fill_mixer(entry, high, low):
    rows, columns = high.shape
    lane = lax.broadcasted_iota(jnp.int32, (8, columns), 1)
    row = lax.broadcasted_iota(jnp.int32, (8, columns), 0)
    group = lane // DEPTH
    within = lane - group * DEPTH
    for a in range(rows // DEPTH):
        values = jnp.zeros((8, columns), f32)
        for b in range(columns // DEPTH):
            values = jnp.where(group == b, entry(a, b), values)
        pieces = [jnp.where(within == row + 8 * k, values, 0.0) for k in range(DEPTH // 8)]
        block = jnp.concatenate(pieces, axis=0)
        rounded = block.astype(bf16)
        high[a * DEPTH : (a + 1) * DEPTH, :] = rounded
        low[a * DEPTH : (a + 1) * DEPTH, :] = (block - rounded.astype(f32)).astype(bf16)


def mixed(mixer, fields):
    high, low = mixer
    return jnp.dot(high[...], fields, preferred_element_type=f32) + jnp.dot(
        low[...], fields, preferred_element_type=f32
    )


def tangent_scaled(activity, mixing, own):
    scaled = (1.0 - activity * activity) * mixing
    group = lax.broadcasted_iota(jnp.int32, activity.shape, 0) // DEPTH
    return (scaled + jnp.where(group == own, activity, 0.0)).astype(bf16)


def advance(v, curve, slope, rate, diffusivity, speed):
    return (v.astype(f32) + time_step * (diffusivity * curve - speed * slope + rate)).astype(bf16)


def x_kernel(n, q, params_here, rates, coef, advect, diffuse, state, *rest):
    if q is not None:
        tangent, rest = rest[0], rest[1:]
    d1, d2, filt = rest[:3]
    outs, rest = rest[3 : 3 + n], rest[3 + n :]
    filt_own, rates_high, rates_low, coef_high, coef_low, middle = rest
    me, half = lax.axis_index("pencil"), lax.axis_index("field")
    count, rows, length = state.shape
    fields = outs[0].shape[0]
    size = length // n
    first = half * fields if q is None else 0

    @pl.when(pl.program_id(0) == 0)
    def _():
        fill_mixer(lambda a, b: rates[a, b], rates_high, rates_low)
        fill_mixer(lambda a, b: coef[b, first + a], coef_high, coef_low)
        for r in range(n):
            filt_own[:, r * size : (r + 1) * size] = filt[:, aligned(me ^ r, size)]

    source = state[pl.ds(first, fields)] if q is None else tangent[...]
    own = source.reshape(fields * rows, length)
    for c in range(length // WIDE):
        across = slice(c * WIDE, (c + 1) * WIDE)
        u = state[:, :, across].reshape(count * rows, WIDE)
        activity = jnp.tanh(mixed((rates_high, rates_low), u))
        if q is None:
            scaled = activity.astype(bf16)
        else:
            mixing = mixed((rates_high, rates_low), own[:, across])
            scaled = tangent_scaled(activity, mixing, half * params_here + q)
        rate = mixed((coef_high, coef_low), scaled)
        slope = jnp.dot(own, d1[:, across], preferred_element_type=f32)
        curve = jnp.dot(own, d2[:, across], preferred_element_type=f32)
        for s in range(fields):
            at = slice(s * rows, (s + 1) * rows)
            middle[at, across] = advance(
                own[at, across], curve[at], slope[at], rate[at], diffuse[first + s], advect[0, first + s]
            )
    result = jnp.dot(middle[...], filt_own[...], preferred_element_type=f32).astype(bf16)
    for r in range(n):
        outs[r][...] = result[:, r * size : (r + 1) * size].reshape(fields, rows, size)


def y_kernel(n, q, params_here, rates, coef, advect, diffuse, *rest):
    own, rest = rest[:n], rest[n:]
    other, rest = rest[:n], rest[n:]
    if q is None:
        arrived = own
    else:
        arrived, rest = rest[:n], rest[n:]
    d1t, d2t, filtt = rest[:3]
    outs, rest = rest[3 : 3 + n], rest[3 + n :]
    filt_own, v_full, rate_full, state_high, state_low, coef_high, coef_low = rest[:7]
    me, half = lax.axis_index("pencil"), lax.axis_index("field")
    here = own[0].shape[0]
    count = rates.shape[1]
    size = own[0].shape[1]
    fields = outs[0].shape[0]
    first = half * here if q is None else 0

    fill_mixer(lambda a, b: rates[a, lax.rem(half * here + b, count)], state_high, state_low)
    fill_mixer(lambda a, b: coef[b, first + a], coef_high, coef_low)
    if q is not None:
        rates_high, rates_low = rest[7:]
        fill_mixer(lambda a, b: rates[a, b], rates_high, rates_low)

    def tile(refs, down):
        return jnp.concatenate([ref[:, down, :].reshape(ref.shape[0] * DEPTH, size) for ref in refs], axis=0)

    def pair(refs, j):
        starts = [(2 * j + k) * DEPTH for k in range(2)]
        return jnp.concatenate([tile(refs, pl.ds(pl.multiple_of(at, DEPTH), DEPTH)) for at in starts], axis=1)

    for r in range(n):
        filt_own[r * size : (r + 1) * size, :] = filtt[aligned(me ^ r, size), :]
        for s in range(fields):
            v_full[aligned(me ^ r, size), s * size : (s + 1) * size] = arrived[r][s]

        def rate_block(j, carry, r=r):
            activity = jnp.tanh(mixed((state_high, state_low), pair((own[r], other[r]), j)))
            if q is None:
                scaled = activity.astype(bf16)
            else:
                mixing = mixed((rates_high, rates_low), pair((arrived[r],), j))
                scaled = tangent_scaled(activity, mixing, half * params_here + q)
            rate = mixed((coef_high, coef_low), scaled)
            for k in range(2):
                down = pl.ds(pl.multiple_of((me ^ r) * size + (2 * j + k) * DEPTH, DEPTH), DEPTH)
                for s in range(fields):
                    rate_full[down, s * size : (s + 1) * size] = rate[
                        s * DEPTH : (s + 1) * DEPTH, k * size : (k + 1) * size
                    ]
            return carry

        lax.fori_loop(0, size // (2 * DEPTH), rate_block, 0)

    def two_fields(f, carry):
        v = v_full[:, aligned(f, 2 * size)]
        slope = jnp.dot(d1t[...], v, preferred_element_type=f32)
        curve = jnp.dot(d2t[...], v, preferred_element_type=f32)
        columns = []
        for k in range(2):
            s = 2 * f + k
            across = slice(k * size, (k + 1) * size)
            columns.append(
                advance(
                    v[:, across],
                    curve[:, across],
                    slope[:, across],
                    rate_full[:, aligned(s, size)],
                    diffuse[first + s],
                    advect[1, first + s],
                )
            )
        middle = jnp.concatenate(columns, axis=1)
        result = jnp.dot(filt_own[...], middle, preferred_element_type=f32).astype(bf16)
        for r in range(n):
            for k in range(2):
                outs[r][2 * f + k] = result[r * size : (r + 1) * size, k * size : (k + 1) * size]
        return carry

    lax.fori_loop(0, fields // 2, two_fields, 0)


def place_kernel(n, slots_of, *rest):
    me, half = lax.axis_index("pencil"), lax.axis_index("field")
    out = rest[-1]
    slots = rest[: n * slots_of]
    here = slots[0].shape[0]
    size = slots[0].shape[2]
    for g in range(slots_of):
        for r in range(n):
            slot = slots[g * n + r]
            for s in range(here):
                if slots_of == 1:
                    out[0, s, 0, :, aligned(me ^ r, size)] = slot[s]
                else:
                    at = (half if g == 0 else 1 - half) * here + s
                    out[at, 0, :, aligned(me ^ r, size)] = slot[s]


SMEM = pl.BlockSpec(memory_space=pltpu.SMEM)
VMEM = pl.BlockSpec(memory_space=pltpu.VMEM)
HBM = pl.BlockSpec(memory_space=pl.ANY)


def cost(flops, moved):
    return pl.CostEstimate(flops=flops, bytes_accessed=moved, transcendentals=0)


def mixers(fields, count):
    return [pltpu.VMEM((fields * DEPTH, count * DEPTH), bf16)] * 2


def x_call(n, q, scalars, state, tangents, d1, d2, filt, here):
    count, _, deep, length = state.shape
    size = length // n
    fields = here if q is None else count
    whole = pl.BlockSpec((length, length), lambda i: (0, 0))
    arrays = [state]
    specs = [pl.BlockSpec((count, None, DEPTH, length), lambda i: (0, 0, i, 0))]
    if q is not None:
        arrays.append(tangents)
        specs.append(pl.BlockSpec((None, count, None, DEPTH, length), lambda i: (q, 0, 0, i, 0)))
    return pl.pallas_call(
        functools.partial(x_kernel, n, q, None if q is None else tangents.shape[0]),
        grid=(deep // DEPTH,),
        out_shape=[jax.ShapeDtypeStruct((fields, deep, size), bf16)] * n,
        in_specs=[SMEM] * 4 + specs + [whole] * 3,
        out_specs=[pl.BlockSpec((fields, DEPTH, size), lambda i: (0, i, 0))] * n,
        scratch_shapes=[pltpu.VMEM((length, length), bf16)]
        + mixers(count, count)
        + mixers(fields, count)
        + [pltpu.VMEM((fields * DEPTH, length), bf16)],
        cost_estimate=cost(6 * fields * deep * length * length, 4 * fields * deep * length),
        name="x_state" if q is None else f"x_tangent{q}",
    )(*scalars, *arrays, d1, d2, filt)


def y_call(n, q, params_here, scalars, own, other, arrived, turned):
    here, deep, size = own[0].shape
    count = scalars[0].shape[1]
    length = deep * n
    fields = here if q is None else count
    arrays = list(own) + list(other) + list(arrived or ())
    return pl.pallas_call(
        functools.partial(y_kernel, n, q, params_here),
        out_shape=[jax.ShapeDtypeStruct((fields, deep, size), bf16)] * n,
        in_specs=[SMEM] * 4 + [VMEM] * (len(arrays) + 3),
        out_specs=[VMEM] * n,
        scratch_shapes=[
            pltpu.VMEM((length, length), bf16),
            pltpu.VMEM((length, fields * size), bf16),
            pltpu.VMEM((length, fields * size), f32),
        ]
        + mixers(count, count)
        + mixers(fields, count)
        + ([] if q is None else mixers(count, count)),
        cost_estimate=cost(6 * fields * deep * length * length, 4 * fields * deep * length),
        name="y_state" if q is None else f"y_tangent{q}",
    )(*scalars, *arrays, *turned)


def place_state(n, shape, own, other):
    return pl.pallas_call(
        functools.partial(place_kernel, n, 2),
        out_shape=jax.ShapeDtypeStruct(shape, bf16),
        in_specs=[VMEM] * (2 * n),
        out_specs=VMEM,
        name="place_state",
    )(*own, *other)


def place_tangent(n, q, shape, slots, buffer):
    count, deep, size = slots[0].shape
    part = 2
    specs = [pl.BlockSpec((part, deep, size), lambda i: (i, 0, 0))] * n
    arrays = list(slots)
    aliases = {}
    if buffer is not None:
        specs.append(HBM)
        arrays.append(buffer)
        aliases = {n: 0}
    return pl.pallas_call(
        functools.partial(place_kernel, n, 1),
        grid=(count // part,),
        out_shape=jax.ShapeDtypeStruct(shape, bf16),
        in_specs=specs,
        out_specs=pl.BlockSpec((1, part, 1, deep, shape[-1]), lambda i: (q, i, 0, 0, 0)),
        input_output_aliases=aliases,
        name=f"place_tangent{q}",
    )(*arrays)


def exchange(n, slots):
    order = list(range(n // 2, n)) + list(range(1, n // 2))
    arrived = {r: lax.ppermute(slots[r], "pencil", [(i, i ^ r) for i in range(n)]) for r in order}
    return [slots[0]] + [arrived[r] for r in range(1, n)]


def swap(slots):
    return [lax.ppermute(slot, "field", [(0, 1), (1, 0)]) for slot in slots]


def pipelined(n, state, tangents, d1, d2, filt, advect, diffuse, coef, rates):
    params_here = tangents.shape[0]
    here = state.shape[0] // 2
    scalars = (rates, coef, advect, diffuse)
    own = exchange(n, x_call(n, None, scalars, state, None, d1, d2, filt, here))
    sent = [
        exchange(n, x_call(n, q, scalars, state, tangents, d1, d2, filt, here)) for q in range(params_here)
    ]
    turned = (d1.T, d2.T, filt.T)
    other = swap(own)
    mine = exchange(n, y_call(n, None, params_here, scalars, own, other, None, turned))
    buffer = None
    for q in range(params_here):
        back = exchange(n, y_call(n, q, params_here, scalars, own, other, sent[q], turned))
        buffer = place_tangent(n, q, tangents.shape, back, buffer)
    return (place_state(n, state.shape, mine, swap(mine)), buffer)


def solution(mesh):
    in_specs = (
        P("parts", "slab", "pencil", None),
        P(("parts", "field"), None, "slab", "pencil", None),
        P(),
        P(),
        P(),
        P(),
        P(),
        P(),
        P(),
    )
    out_specs = (
        P("parts", "slab", "pencil", None),
        P(("parts", "field"), None, "slab", "pencil", None),
    )
    n = mesh.shape["pencil"]

    def local(state, tangents, *others):
        count, planes, deep, length = state.shape
        fits = (
            n & (n - 1) == 0
            and mesh.shape["field"] == 2
            and count * DEPTH == WIDE
            and others[-1].shape[0] == count
            and tangents.shape[0] * 2 == count
            and length % WIDE == 0
            and planes == 1
            and deep == LANES
            and deep * n == length
        )
        if fits:
            return pipelined(n, state, tangents, *others)
        return plain(state, tangents, *others)

    return jax.shard_map(local, mesh=mesh, in_specs=in_specs, out_specs=out_specs, check_vma=False)
```

```python
import functools

import jax
import jax.numpy as jnp
from jax import lax
from jax.experimental import pallas as pl
from jax.experimental.pallas import tpu as pltpu
from jax.sharding import PartitionSpec as P


highest = lax.Precision.HIGHEST
time_step = 0.4
f32 = jnp.float32
bf16 = jnp.bfloat16
LANES = 128
WIDE = 2 * LANES
DEPTH = 32


def spread(values, fields):
    return values.reshape(values.shape + (1,) * (fields.ndim - values.ndim))


def reaction(state, tangent, coef, rates, offset):
    state_float = state.astype(f32)
    argument = jnp.einsum("ps,s...->p...", rates, state_float, precision=highest)
    activity = jnp.tanh(argument)
    slopes = 1.0 - activity * activity
    state_rate = jnp.einsum("ps,p...->s...", coef, activity, precision=highest)
    tangent_float = tangent.astype(f32)
    mixing = jnp.einsum("pt,qt...->qp...", rates, tangent_float, precision=highest)
    number = tangent.shape[0]
    own_coef = lax.dynamic_slice_in_dim(coef, offset, number, 0)
    own_activity = lax.dynamic_slice_in_dim(activity, offset, number, 0)
    tangent_rate = jnp.einsum("ps,qp...->qs...", coef, slopes[None] * mixing, precision=highest)
    tangent_rate = tangent_rate + spread(own_coef, tangent) * own_activity[:, None]
    return (state_rate, tangent_rate)


def update(fields, rate, speeds, diffusivity, operators):
    derivative_op, diffusion_op, filter_op = operators
    slope_term = jnp.dot(fields, derivative_op, preferred_element_type=f32)
    curve_term = jnp.dot(fields, diffusion_op, preferred_element_type=f32)
    middle = fields.astype(f32) + time_step * (
        spread(diffusivity, fields) * curve_term - spread(speeds, fields) * slope_term + rate
    )
    middle = middle.astype(bf16)
    return jnp.dot(middle, filter_op, preferred_element_type=f32).astype(bf16)


def plain(state, tangents, d1, d2, filt, advect, diffuse, coef, rates):
    params_here = tangents.shape[0]
    state_count = state.shape[0]
    offset = lax.axis_index("field") * params_here
    operators = (d1, d2, filt)
    for direction in range(2):
        speeds = advect[direction]
        state_rate, tangent_rate = reaction(state, tangents, coef, rates, offset)
        tangents = update(tangents, tangent_rate, speeds[None, :], diffuse[None, :], operators)
        outgoing = update(state, state_rate, speeds, diffuse, operators)
        merged = tangents.reshape((params_here * state_count,) + tangents.shape[2:])
        arrived = lax.all_to_all(outgoing, "pencil", split_axis=3, concat_axis=2, tiled=True)
        merged = lax.all_to_all(merged, "pencil", split_axis=3, concat_axis=2, tiled=True)
        state = jnp.swapaxes(arrived, 2, 3)
        merged = jnp.swapaxes(merged, 2, 3)
        tangents = merged.reshape((params_here, state_count) + merged.shape[1:])
    return (state, tangents)


def aligned(index, size):
    return pl.ds(pl.multiple_of(index * size, size), size)


def fill_mixer(entry, high, low):
    rows, columns = high.shape
    lane = lax.broadcasted_iota(jnp.int32, (8, columns), 1)
    row = lax.broadcasted_iota(jnp.int32, (8, columns), 0)
    group = lane // DEPTH
    within = lane - group * DEPTH
    for a in range(rows // DEPTH):
        values = jnp.zeros((8, columns), f32)
        for b in range(columns // DEPTH):
            values = jnp.where(group == b, entry(a, b), values)
        pieces = [jnp.where(within == row + 8 * k, values, 0.0) for k in range(DEPTH // 8)]
        block = jnp.concatenate(pieces, axis=0)
        rounded = block.astype(bf16)
        high[a * DEPTH : (a + 1) * DEPTH, :] = rounded
        low[a * DEPTH : (a + 1) * DEPTH, :] = (block - rounded.astype(f32)).astype(bf16)


def mixed(mixer, fields):
    high, low = mixer
    return jnp.dot(high[...], fields, preferred_element_type=f32) + jnp.dot(
        low[...], fields, preferred_element_type=f32
    )


def mixed_float(mixer, values):
    rounded = values.astype(bf16)
    left = (values - rounded.astype(f32)).astype(bf16)
    return mixed(mixer, rounded) + jnp.dot(mixer[0][...], left, preferred_element_type=f32)


def tangent_scaled(activity, mixing, own):
    scaled = (1.0 - activity * activity) * mixing
    group = lax.broadcasted_iota(jnp.int32, activity.shape, 0) // DEPTH
    return scaled + jnp.where(group == own, activity, 0.0)


def advance(v, curve, slope, rate, diffusivity, speed):
    return (v.astype(f32) + time_step * (diffusivity * curve - speed * slope + rate)).astype(bf16)


def x_kernel(n, q, params_here, rates, coef, advect, diffuse, state, *rest):
    if q is not None:
        tangent, rest = rest[0], rest[1:]
    d1, d2, filt = rest[:3]
    outs, rest = rest[3 : 3 + n], rest[3 + n :]
    filt_own, rates_high, rates_low, coef_high, coef_low, middle = rest
    me, half = lax.axis_index("pencil"), lax.axis_index("field")
    count, rows, length = state.shape
    fields = outs[0].shape[0]
    size = length // n
    first = half * fields if q is None else 0

    @pl.when(pl.program_id(0) == 0)
    def _():
        fill_mixer(lambda a, b: rates[a, b], rates_high, rates_low)
        fill_mixer(lambda a, b: coef[b, first + a], coef_high, coef_low)
        for r in range(n):
            filt_own[:, r * size : (r + 1) * size] = filt[:, aligned(me ^ r, size)]

    source = state[pl.ds(first, fields)] if q is None else tangent[...]
    own = source.reshape(fields * rows, length)
    for c in range(length // WIDE):
        across = slice(c * WIDE, (c + 1) * WIDE)
        u = state[:, :, across].reshape(count * rows, WIDE)
        activity = jnp.tanh(mixed((rates_high, rates_low), u))
        if q is None:
            scaled = activity
        else:
            mixing = mixed((rates_high, rates_low), own[:, across])
            scaled = tangent_scaled(activity, mixing, half * params_here + q)
        rate = mixed_float((coef_high, coef_low), scaled)
        slope = jnp.dot(own, d1[:, across], preferred_element_type=f32)
        curve = jnp.dot(own, d2[:, across], preferred_element_type=f32)
        for s in range(fields):
            at = slice(s * rows, (s + 1) * rows)
            middle[at, across] = advance(
                own[at, across], curve[at], slope[at], rate[at], diffuse[first + s], advect[0, first + s]
            )
    result = jnp.dot(middle[...], filt_own[...], preferred_element_type=f32).astype(bf16)
    for r in range(n):
        outs[r][...] = result[:, r * size : (r + 1) * size].reshape(fields, rows, size)


def y_kernel(n, q, params_here, rates, coef, advect, diffuse, *rest):
    own, rest = rest[:n], rest[n:]
    other, rest = rest[:n], rest[n:]
    if q is None:
        arrived = own
    else:
        arrived, rest = rest[:n], rest[n:]
    d1t, d2t, filtt = rest[:3]
    outs, rest = rest[3 : 3 + n], rest[3 + n :]
    filt_own, v_full, rate_full, state_high, state_low, coef_high, coef_low = rest[:7]
    me, half = lax.axis_index("pencil"), lax.axis_index("field")
    here = own[0].shape[0]
    count = rates.shape[1]
    size = own[0].shape[1]
    fields = outs[0].shape[0]
    first = half * here if q is None else 0

    fill_mixer(lambda a, b: rates[a, lax.rem(half * here + b, count)], state_high, state_low)
    fill_mixer(lambda a, b: coef[b, first + a], coef_high, coef_low)
    if q is not None:
        rates_high, rates_low = rest[7:]
        fill_mixer(lambda a, b: rates[a, b], rates_high, rates_low)

    def tile(refs, down):
        return jnp.concatenate([ref[:, down, :].reshape(ref.shape[0] * DEPTH, size) for ref in refs], axis=0)

    def pair(refs, j):
        starts = [(2 * j + k) * DEPTH for k in range(2)]
        return jnp.concatenate([tile(refs, pl.ds(pl.multiple_of(at, DEPTH), DEPTH)) for at in starts], axis=1)

    for r in range(n):
        filt_own[r * size : (r + 1) * size, :] = filtt[aligned(me ^ r, size), :]
        for s in range(fields):
            v_full[aligned(me ^ r, size), s * size : (s + 1) * size] = arrived[r][s]

        def rate_block(j, carry, r=r):
            activity = jnp.tanh(mixed((state_high, state_low), pair((own[r], other[r]), j)))
            if q is None:
                scaled = activity
            else:
                mixing = mixed((rates_high, rates_low), pair((arrived[r],), j))
                scaled = tangent_scaled(activity, mixing, half * params_here + q)
            rate = mixed_float((coef_high, coef_low), scaled)
            for k in range(2):
                down = pl.ds(pl.multiple_of((me ^ r) * size + (2 * j + k) * DEPTH, DEPTH), DEPTH)
                for s in range(fields):
                    rate_full[down, s * size : (s + 1) * size] = rate[
                        s * DEPTH : (s + 1) * DEPTH, k * size : (k + 1) * size
                    ]
            return carry

        lax.fori_loop(0, size // (2 * DEPTH), rate_block, 0)

    def two_fields(f, carry):
        v = v_full[:, aligned(f, 2 * size)]
        slope = jnp.dot(d1t[...], v, preferred_element_type=f32)
        curve = jnp.dot(d2t[...], v, preferred_element_type=f32)
        columns = []
        for k in range(2):
            s = 2 * f + k
            across = slice(k * size, (k + 1) * size)
            columns.append(
                advance(
                    v[:, across],
                    curve[:, across],
                    slope[:, across],
                    rate_full[:, aligned(s, size)],
                    diffuse[first + s],
                    advect[1, first + s],
                )
            )
        middle = jnp.concatenate(columns, axis=1)
        result = jnp.dot(filt_own[...], middle, preferred_element_type=f32).astype(bf16)
        for r in range(n):
            for k in range(2):
                outs[r][2 * f + k] = result[r * size : (r + 1) * size, k * size : (k + 1) * size]
        return carry

    lax.fori_loop(0, fields // 2, two_fields, 0)


def place_kernel(n, slots_of, *rest):
    me, half = lax.axis_index("pencil"), lax.axis_index("field")
    out = rest[-1]
    slots = rest[: n * slots_of]
    here = slots[0].shape[0]
    size = slots[0].shape[2]
    for g in range(slots_of):
        for r in range(n):
            slot = slots[g * n + r]
            for s in range(here):
                if slots_of == 1:
                    out[0, s, 0, :, aligned(me ^ r, size)] = slot[s]
                else:
                    at = (half if g == 0 else 1 - half) * here + s
                    out[at, 0, :, aligned(me ^ r, size)] = slot[s]


SMEM = pl.BlockSpec(memory_space=pltpu.SMEM)
VMEM = pl.BlockSpec(memory_space=pltpu.VMEM)
HBM = pl.BlockSpec(memory_space=pl.ANY)
GRANT = pltpu.CompilerParams(vmem_limit_bytes=32 * 1024 * 1024)


def cost(flops, moved):
    return pl.CostEstimate(flops=flops, bytes_accessed=moved, transcendentals=0)


def mixers(fields, count):
    return [pltpu.VMEM((fields * DEPTH, count * DEPTH), bf16)] * 2


def x_call(n, q, scalars, state, tangents, d1, d2, filt, here):
    count, _, deep, length = state.shape
    size = length // n
    fields = here if q is None else count
    whole = pl.BlockSpec((length, length), lambda i: (0, 0))
    arrays = [state]
    specs = [pl.BlockSpec((count, None, DEPTH, length), lambda i: (0, 0, i, 0))]
    if q is not None:
        arrays.append(tangents)
        specs.append(pl.BlockSpec((None, count, None, DEPTH, length), lambda i: (q, 0, 0, i, 0)))
    return pl.pallas_call(
        functools.partial(x_kernel, n, q, None if q is None else tangents.shape[0]),
        grid=(deep // DEPTH,),
        out_shape=[jax.ShapeDtypeStruct((fields, deep, size), bf16)] * n,
        in_specs=[SMEM] * 4 + specs + [whole] * 3,
        out_specs=[pl.BlockSpec((fields, DEPTH, size), lambda i: (0, i, 0))] * n,
        scratch_shapes=[pltpu.VMEM((length, length), bf16)]
        + mixers(count, count)
        + mixers(fields, count)
        + [pltpu.VMEM((fields * DEPTH, length), bf16)],
        cost_estimate=cost(6 * fields * deep * length * length, 4 * fields * deep * length),
    )(*scalars, *arrays, d1, d2, filt)


def y_call(n, q, params_here, scalars, own, other, arrived, turned):
    here, deep, size = own[0].shape
    count = scalars[0].shape[1]
    length = deep * n
    fields = here if q is None else count
    arrays = list(own) + list(other) + list(arrived or ())
    return pl.pallas_call(
        functools.partial(y_kernel, n, q, params_here),
        out_shape=[jax.ShapeDtypeStruct((fields, deep, size), bf16)] * n,
        in_specs=[SMEM] * 4 + [VMEM] * (len(arrays) + 3),
        out_specs=[VMEM] * n,
        scratch_shapes=[
            pltpu.VMEM((length, length), bf16),
            pltpu.VMEM((length, fields * size), bf16),
            pltpu.VMEM((length, fields * size), f32),
        ]
        + mixers(count, count)
        + mixers(fields, count)
        + ([] if q is None else mixers(count, count)),
        compiler_params=GRANT,
        cost_estimate=cost(6 * fields * deep * length * length, 4 * fields * deep * length),
    )(*scalars, *arrays, *turned)


def place_state(n, shape, own, other):
    return pl.pallas_call(
        functools.partial(place_kernel, n, 2),
        out_shape=jax.ShapeDtypeStruct(shape, bf16),
        in_specs=[VMEM] * (2 * n),
        out_specs=VMEM,
        compiler_params=GRANT,
        name="place_state",
    )(*own, *other)


def place_tangent(n, q, shape, slots, buffer):
    count, deep, size = slots[0].shape
    part = 2
    specs = [pl.BlockSpec((part, deep, size), lambda i: (i, 0, 0))] * n
    arrays = list(slots)
    aliases = {}
    if buffer is not None:
        specs.append(HBM)
        arrays.append(buffer)
        aliases = {n: 0}
    return pl.pallas_call(
        functools.partial(place_kernel, n, 1),
        grid=(count // part,),
        out_shape=jax.ShapeDtypeStruct(shape, bf16),
        in_specs=specs,
        out_specs=pl.BlockSpec((1, part, 1, deep, shape[-1]), lambda i: (q, i, 0, 0, 0)),
        input_output_aliases=aliases,
        compiler_params=GRANT,
    )(*arrays)


def exchange(n, slots):
    order = list(range(n // 2, n)) + list(range(1, n // 2))
    arrived = {r: lax.ppermute(slots[r], "pencil", [(i, i ^ r) for i in range(n)]) for r in order}
    return [slots[0]] + [arrived[r] for r in range(1, n)]


def swap(slots):
    return [lax.ppermute(slot, "field", [(0, 1), (1, 0)]) for slot in slots]


def pipelined(n, state, tangents, d1, d2, filt, advect, diffuse, coef, rates):
    params = range(tangents.shape[0])
    here = state.shape[0] // 2
    scalars = (rates, coef, advect, diffuse)

    def forth(q):
        return x_call(n, q, scalars, state, tangents, d1, d2, filt, here)

    own = exchange(n, forth(None))
    sent = [exchange(n, forth(q)) for q in params]
    turned = (d1.T, d2.T, filt.T)
    other = swap(own)

    def turn(q):
        return y_call(n, q, len(params), scalars, own, other, None if q is None else sent[q], turned)

    mine = exchange(n, turn(None))
    theirs = swap(mine)
    buffer = None
    for q in params:
        back = exchange(n, turn(q))
        buffer = place_tangent(n, q, tangents.shape, back, buffer)
    return (place_state(n, state.shape, mine, theirs), buffer)


def solution(mesh):
    in_specs = (
        P("parts", "slab", "pencil", None),
        P(("parts", "field"), None, "slab", "pencil", None),
        P(),
        P(),
        P(),
        P(),
        P(),
        P(),
        P(),
    )
    out_specs = (
        P("parts", "slab", "pencil", None),
        P(("parts", "field"), None, "slab", "pencil", None),
    )
    n = mesh.shape["pencil"]

    def step(state, tangents, *others):
        count, planes, _, length = state.shape
        count //= mesh.shape["parts"]
        params_here = tangents.shape[0] // (mesh.shape["parts"] * mesh.shape["field"])
        fits = (
            n & (n - 1) == 0
            and mesh.shape["field"] == 2
            and count * DEPTH == WIDE
            and others[-1].shape[0] == count
            and params_here * 2 == count
            and planes == mesh.shape["slab"]
            and n * LANES == length == state.shape[2]
            and length % WIDE == 0
        )
        local = functools.partial(pipelined, n) if fits else plain
        call = jax.shard_map(local, mesh=mesh, in_specs=in_specs, out_specs=out_specs, check_vma=False)
        return call(state, tangents, *others)

    return step
```

```python
import functools

import jax
import jax.numpy as jnp
from jax import lax
from jax.experimental import pallas as pl
from jax.experimental.pallas import tpu as pltpu
from jax.sharding import PartitionSpec as P


highest = lax.Precision.HIGHEST
time_step = 0.4
f32 = jnp.float32
bf16 = jnp.bfloat16
LANES = 128
WIDE = 2 * LANES
DEPTH = 32


def spread(values, fields):
    return values.reshape(values.shape + (1,) * (fields.ndim - values.ndim))


def reaction(state, tangent, coef, rates, offset):
    state_float = state.astype(f32)
    argument = jnp.einsum("ps,s...->p...", rates, state_float, precision=highest)
    activity = jnp.tanh(argument)
    slopes = 1.0 - activity * activity
    state_rate = jnp.einsum("ps,p...->s...", coef, activity, precision=highest)
    tangent_float = tangent.astype(f32)
    mixing = jnp.einsum("pt,qt...->qp...", rates, tangent_float, precision=highest)
    number = tangent.shape[0]
    own_coef = lax.dynamic_slice_in_dim(coef, offset, number, 0)
    own_activity = lax.dynamic_slice_in_dim(activity, offset, number, 0)
    tangent_rate = jnp.einsum("ps,qp...->qs...", coef, slopes[None] * mixing, precision=highest)
    tangent_rate = tangent_rate + spread(own_coef, tangent) * own_activity[:, None]
    return (state_rate, tangent_rate)


def update(fields, rate, speeds, diffusivity, operators):
    derivative_op, diffusion_op, filter_op = operators
    slope_term = jnp.dot(fields, derivative_op, preferred_element_type=f32)
    curve_term = jnp.dot(fields, diffusion_op, preferred_element_type=f32)
    middle = fields.astype(f32) + time_step * (
        spread(diffusivity, fields) * curve_term - spread(speeds, fields) * slope_term + rate
    )
    middle = middle.astype(bf16)
    return jnp.dot(middle, filter_op, preferred_element_type=f32).astype(bf16)


def plain(state, tangents, d1, d2, filt, advect, diffuse, coef, rates):
    params_here = tangents.shape[0]
    state_count = state.shape[0]
    offset = lax.axis_index("field") * params_here
    operators = (d1, d2, filt)
    for direction in range(2):
        speeds = advect[direction]
        state_rate, tangent_rate = reaction(state, tangents, coef, rates, offset)
        tangents = update(tangents, tangent_rate, speeds[None, :], diffuse[None, :], operators)
        outgoing = update(state, state_rate, speeds, diffuse, operators)
        merged = tangents.reshape((params_here * state_count,) + tangents.shape[2:])
        arrived = lax.all_to_all(outgoing, "pencil", split_axis=3, concat_axis=2, tiled=True)
        merged = lax.all_to_all(merged, "pencil", split_axis=3, concat_axis=2, tiled=True)
        state = jnp.swapaxes(arrived, 2, 3)
        merged = jnp.swapaxes(merged, 2, 3)
        tangents = merged.reshape((params_here, state_count) + merged.shape[1:])
    return (state, tangents)


def aligned(index, size):
    return pl.ds(pl.multiple_of(index * size, size), size)


def fill_mixer(entry, high, low):
    rows, columns = high.shape
    lane = lax.broadcasted_iota(jnp.int32, (8, columns), 1)
    row = lax.broadcasted_iota(jnp.int32, (8, columns), 0)
    group = lane // DEPTH
    within = lane - group * DEPTH
    for a in range(rows // DEPTH):
        values = jnp.zeros((8, columns), f32)
        for b in range(columns // DEPTH):
            values = jnp.where(group == b, entry(a, b), values)
        pieces = [jnp.where(within == row + 8 * k, values, 0.0) for k in range(DEPTH // 8)]
        block = jnp.concatenate(pieces, axis=0)
        rounded = block.astype(bf16)
        high[a * DEPTH : (a + 1) * DEPTH, :] = rounded
        low[a * DEPTH : (a + 1) * DEPTH, :] = (block - rounded.astype(f32)).astype(bf16)


def mixed(mixer, fields):
    high, low = mixer
    return jnp.dot(high[...], fields, preferred_element_type=f32) + jnp.dot(
        low[...], fields, preferred_element_type=f32
    )


def mixed_float(mixer, values):
    rounded = values.astype(bf16)
    left = (values - rounded.astype(f32)).astype(bf16)
    return mixed(mixer, rounded) + jnp.dot(mixer[0][...], left, preferred_element_type=f32)


def tangent_scaled(activity, mixing, own):
    scaled = (1.0 - activity * activity) * mixing
    group = lax.broadcasted_iota(jnp.int32, activity.shape, 0) // DEPTH
    return scaled + jnp.where(group == own, activity, 0.0)


def advance(v, curve, slope, rate, diffusivity, speed):
    return (v.astype(f32) + time_step * (diffusivity * curve - speed * slope + rate)).astype(bf16)


def x_state_kernel(n, rates, coef, advect, diffuse, state_far, d1_far, d2_far, filt_far, *rest):
    outs, rest = rest[:n], rest[n:]
    state, d1, d2, filt, filt_own, rates_high, rates_low, rate, middle, sems = rest
    copies = [
        pltpu.make_async_copy(far, near, sems.at[i])
        for i, (far, near) in enumerate(
            [(state_far, state), (d1_far, d1), (d2_far, d2), (filt_far, filt)]
        )
    ]
    for copy in copies:
        copy.start()
    me, half = lax.axis_index("pencil"), lax.axis_index("field")
    count, _, rows, length = state.shape
    fields = outs[0].shape[0]
    size = length // n
    first = half * fields
    fill_mixer(lambda a, b: rates[a, b], rates_high, rates_low)
    copies[0].wait()
    for j in range(rows // DEPTH):
        down = slice(j * DEPTH, (j + 1) * DEPTH)
        for c in range(length // WIDE):
            across = slice(c * WIDE, (c + 1) * WIDE)
            u = state[:, 0, down, across].reshape(count * DEPTH, WIDE)
            activity = jnp.tanh(mixed((rates_high, rates_low), u))
            for s in range(fields):
                total = None
                for p in range(rates.shape[0]):
                    term = coef[p, first + s] * activity[p * DEPTH : (p + 1) * DEPTH]
                    total = term if total is None else total + term
                rate[s * rows + j * DEPTH : s * rows + (j + 1) * DEPTH, across] = total
    own = state[pl.ds(first, fields), 0].reshape(fields * rows, length)
    copies[1].wait()
    copies[2].wait()
    for c in range(length // WIDE):
        across = slice(c * WIDE, (c + 1) * WIDE)
        slope = jnp.dot(own, d1[:, across], preferred_element_type=f32)
        curve = jnp.dot(own, d2[:, across], preferred_element_type=f32)
        for s in range(fields):
            at = slice(s * rows, (s + 1) * rows)
            middle[at, across] = advance(
                own[at, across], curve[at], slope[at], rate[at, across], diffuse[first + s], advect[0, first + s]
            )
    copies[3].wait()
    for r in range(n):
        filt_own[:, r * size : (r + 1) * size] = filt[:, aligned(me ^ r, size)]
    result = jnp.dot(middle[...], filt_own[...], preferred_element_type=f32).astype(bf16)
    for r in range(n):
        outs[r][...] = result[:, r * size : (r + 1) * size].reshape(fields, rows, size)


def x_kernel(n, q, params_here, rates, coef, advect, diffuse, state, tangent, d1, d2, filt, *rest):
    outs, rest = rest[:n], rest[n:]
    filt_own, rates_high, rates_low, coef_high, coef_low, middle = rest
    me, half = lax.axis_index("pencil"), lax.axis_index("field")
    count, rows, length = state.shape
    size = length // n

    @pl.when(pl.program_id(0) == 0)
    def _():
        fill_mixer(lambda a, b: rates[a, b], rates_high, rates_low)
        fill_mixer(lambda a, b: coef[b, a], coef_high, coef_low)
        for r in range(n):
            filt_own[:, r * size : (r + 1) * size] = filt[:, aligned(me ^ r, size)]

    own = tangent[...].reshape(count * rows, length)
    for c in range(length // WIDE):
        across = slice(c * WIDE, (c + 1) * WIDE)
        u = state[:, :, across].reshape(count * rows, WIDE)
        activity = jnp.tanh(mixed((rates_high, rates_low), u))
        mixing = mixed((rates_high, rates_low), own[:, across])
        scaled = tangent_scaled(activity, mixing, half * params_here + q)
        rate = mixed_float((coef_high, coef_low), scaled)
        slope = jnp.dot(own, d1[:, across], preferred_element_type=f32)
        curve = jnp.dot(own, d2[:, across], preferred_element_type=f32)
        for s in range(count):
            at = slice(s * rows, (s + 1) * rows)
            middle[at, across] = advance(
                own[at, across], curve[at], slope[at], rate[at], diffuse[s], advect[0, s]
            )
    result = jnp.dot(middle[...], filt_own[...], preferred_element_type=f32).astype(bf16)
    for r in range(n):
        outs[r][...] = result[:, r * size : (r + 1) * size].reshape(count, rows, size)


def y_kernel(n, q, params_here, rates, coef, advect, diffuse, *rest):
    own, rest = rest[:n], rest[n:]
    other, rest = rest[:n], rest[n:]
    if q is None:
        arrived = own
    else:
        arrived, rest = rest[:n], rest[n:]
    d1t, d2t, filtt = rest[:3]
    outs, rest = rest[3 : 3 + n], rest[3 + n :]
    filt_own, v_full, rate_full, state_high, state_low, coef_high, coef_low = rest[:7]
    me, half = lax.axis_index("pencil"), lax.axis_index("field")
    here = own[0].shape[0]
    count = rates.shape[1]
    size = own[0].shape[1]
    fields = outs[0].shape[0]
    first = half * here if q is None else 0

    fill_mixer(lambda a, b: rates[a, lax.rem(half * here + b, count)], state_high, state_low)
    fill_mixer(lambda a, b: coef[b, first + a], coef_high, coef_low)
    if q is not None:
        rates_high, rates_low = rest[7:]
        fill_mixer(lambda a, b: rates[a, b], rates_high, rates_low)

    def tile(refs, down):
        return jnp.concatenate([ref[:, down, :].reshape(ref.shape[0] * DEPTH, size) for ref in refs], axis=0)

    def pair(refs, j):
        starts = [(2 * j + k) * DEPTH for k in range(2)]
        return jnp.concatenate([tile(refs, pl.ds(pl.multiple_of(at, DEPTH), DEPTH)) for at in starts], axis=1)

    for r in range(n):
        filt_own[r * size : (r + 1) * size, :] = filtt[aligned(me ^ r, size), :]
        for s in range(fields):
            v_full[aligned(me ^ r, size), s * size : (s + 1) * size] = arrived[r][s]

        def rate_block(j, carry, r=r):
            activity = jnp.tanh(mixed((state_high, state_low), pair((own[r], other[r]), j)))
            if q is None:
                scaled = activity
            else:
                mixing = mixed((rates_high, rates_low), pair((arrived[r],), j))
                scaled = tangent_scaled(activity, mixing, half * params_here + q)
            rate = mixed_float((coef_high, coef_low), scaled)
            for k in range(2):
                down = pl.ds(pl.multiple_of((me ^ r) * size + (2 * j + k) * DEPTH, DEPTH), DEPTH)
                for s in range(fields):
                    rate_full[down, s * size : (s + 1) * size] = rate[
                        s * DEPTH : (s + 1) * DEPTH, k * size : (k + 1) * size
                    ]
            return carry

        lax.fori_loop(0, size // (2 * DEPTH), rate_block, 0)

    def two_fields(f, carry):
        v = v_full[:, aligned(f, 2 * size)]
        slope = jnp.dot(d1t[...], v, preferred_element_type=f32)
        curve = jnp.dot(d2t[...], v, preferred_element_type=f32)
        columns = []
        for k in range(2):
            s = 2 * f + k
            across = slice(k * size, (k + 1) * size)
            columns.append(
                advance(
                    v[:, across],
                    curve[:, across],
                    slope[:, across],
                    rate_full[:, aligned(s, size)],
                    diffuse[first + s],
                    advect[1, first + s],
                )
            )
        middle = jnp.concatenate(columns, axis=1)
        result = jnp.dot(filt_own[...], middle, preferred_element_type=f32).astype(bf16)
        for r in range(n):
            for k in range(2):
                outs[r][2 * f + k] = result[r * size : (r + 1) * size, k * size : (k + 1) * size]
        return carry

    lax.fori_loop(0, fields // 2, two_fields, 0)


def place_kernel(n, q, *rest):
    out, sems = rest[-2:]
    me, half = lax.axis_index("pencil"), lax.axis_index("field")
    groups = 2 if q is None else 1
    copies = []
    for g in range(groups):
        for r in range(n):
            slot = rest[g * n + r]
            here, _, size = slot.shape
            across = aligned(me ^ r, size)
            if q is None:
                target = out.at[aligned(half if g == 0 else 1 - half, here), 0, :, across]
            else:
                target = out.at[q, :, 0, :, across]
            copies.append(pltpu.make_async_copy(slot, target, sems.at[g * n + r]))
    for copy in copies:
        copy.start()
    for copy in copies:
        copy.wait()


SMEM = pl.BlockSpec(memory_space=pltpu.SMEM)
VMEM = pl.BlockSpec(memory_space=pltpu.VMEM)
HBM = pl.BlockSpec(memory_space=pl.ANY)
GRANT = pltpu.CompilerParams(vmem_limit_bytes=32 * 1024 * 1024)


def cost(flops, moved):
    return pl.CostEstimate(flops=flops, bytes_accessed=moved, transcendentals=0)


def mixers(fields, count):
    return [pltpu.VMEM((fields * DEPTH, count * DEPTH), bf16)] * 2


def x_state_call(n, scalars, state, d1, d2, filt, here):
    count, _, deep, length = state.shape
    square = pltpu.VMEM((length, length), bf16)
    return pl.pallas_call(
        functools.partial(x_state_kernel, n),
        out_shape=[jax.ShapeDtypeStruct((here, deep, length // n), bf16)] * n,
        in_specs=[SMEM] * 4 + [HBM] * 4,
        out_specs=[VMEM] * n,
        scratch_shapes=[pltpu.VMEM(state.shape, bf16), square, square, square, square]
        + mixers(count, count)
        + [
            pltpu.VMEM((here * deep, length), f32),
            pltpu.VMEM((here * deep, length), bf16),
            pltpu.SemaphoreType.DMA((4,)),
        ],
        cost_estimate=cost(6 * here * deep * length * length, 4 * here * deep * length),
        name="x_state",
    )(*scalars, state, d1, d2, filt)


def x_call(n, q, scalars, state, tangents, d1, d2, filt):
    params_here, count, _, deep, length = tangents.shape
    size = length // n
    whole = pl.BlockSpec((length, length), lambda i: (0, 0))
    return pl.pallas_call(
        functools.partial(x_kernel, n, q, params_here),
        grid=(deep // DEPTH,),
        out_shape=[jax.ShapeDtypeStruct((count, deep, size), bf16)] * n,
        in_specs=[SMEM] * 4
        + [
            pl.BlockSpec((count, None, DEPTH, length), lambda i: (0, 0, i, 0)),
            pl.BlockSpec((None, count, None, DEPTH, length), lambda i: (q, 0, 0, i, 0)),
        ]
        + [whole] * 3,
        out_specs=[pl.BlockSpec((count, DEPTH, size), lambda i: (0, i, 0))] * n,
        scratch_shapes=[pltpu.VMEM((length, length), bf16)]
        + mixers(count, count) * 2
        + [pltpu.VMEM((count * DEPTH, length), bf16)],
        cost_estimate=cost(6 * count * deep * length * length, 4 * count * deep * length),
    )(*scalars, state, tangents, d1, d2, filt)


def y_call(n, q, params_here, scalars, own, other, arrived, turned):
    here, deep, size = own[0].shape
    count = scalars[0].shape[1]
    length = deep * n
    fields = here if q is None else count
    arrays = list(own) + list(other) + list(arrived or ())
    return pl.pallas_call(
        functools.partial(y_kernel, n, q, params_here),
        out_shape=[jax.ShapeDtypeStruct((fields, deep, size), bf16)] * n,
        in_specs=[SMEM] * 4 + [VMEM] * (len(arrays) + 3),
        out_specs=[VMEM] * n,
        scratch_shapes=[
            pltpu.VMEM((length, length), bf16),
            pltpu.VMEM((length, fields * size), bf16),
            pltpu.VMEM((length, fields * size), f32),
        ]
        + mixers(count, count)
        + mixers(fields, count)
        + ([] if q is None else mixers(count, count)),
        compiler_params=GRANT,
        cost_estimate=cost(6 * fields * deep * length * length, 4 * fields * deep * length),
    )(*scalars, *arrays, *turned)


def place_state(n, shape, own, other):
    return pl.pallas_call(
        functools.partial(place_kernel, n, None),
        out_shape=jax.ShapeDtypeStruct(shape, bf16),
        in_specs=[VMEM] * (2 * n),
        out_specs=HBM,
        scratch_shapes=[pltpu.SemaphoreType.DMA((2 * n,))],
        compiler_params=GRANT,
        name="place_state",
    )(*own, *other)


def place_tangent(n, q, shape, slots, buffer):
    earlier = [] if buffer is None else [buffer]
    return pl.pallas_call(
        functools.partial(place_kernel, n, q),
        out_shape=jax.ShapeDtypeStruct(shape, bf16),
        in_specs=[VMEM] * n + [HBM] * len(earlier),
        out_specs=HBM,
        scratch_shapes=[pltpu.SemaphoreType.DMA((n,))],
        input_output_aliases={n: 0} if earlier else {},
        compiler_params=GRANT,
    )(*slots, *earlier)


def exchange(n, slots):
    order = list(range(n // 2, n)) + list(range(1, n // 2))
    arrived = {r: lax.ppermute(slots[r], "pencil", [(i, i ^ r) for i in range(n)]) for r in order}
    return [slots[0]] + [arrived[r] for r in range(1, n)]


def swap(slots):
    return [lax.ppermute(slot, "field", [(0, 1), (1, 0)]) for slot in slots]


def pipelined(n, state, tangents, d1, d2, filt, advect, diffuse, coef, rates):
    params = range(tangents.shape[0])
    here = state.shape[0] // 2
    scalars = (rates, coef, advect, diffuse)

    def forth(q):
        if q is None:
            return x_state_call(n, scalars, state, d1, d2, filt, here)
        return x_call(n, q, scalars, state, tangents, d1, d2, filt)

    own = exchange(n, forth(None))
    sent = [exchange(n, forth(q)) for q in params]
    turned = (d1.T, d2.T, filt.T)
    other = swap(own)

    def turn(q):
        return y_call(n, q, len(params), scalars, own, other, None if q is None else sent[q], turned)

    mine = exchange(n, turn(None))
    theirs = swap(mine)
    buffer = None
    for q in params:
        back = exchange(n, turn(q))
        buffer = place_tangent(n, q, tangents.shape, back, buffer)
    return (place_state(n, state.shape, mine, theirs), buffer)


def solution(mesh):
    in_specs = (
        P("parts", "slab", "pencil", None),
        P(("parts", "field"), None, "slab", "pencil", None),
        P(),
        P(),
        P(),
        P(),
        P(),
        P(),
        P(),
    )
    out_specs = (
        P("parts", "slab", "pencil", None),
        P(("parts", "field"), None, "slab", "pencil", None),
    )
    n = mesh.shape["pencil"]

    def step(state, tangents, *others):
        count, planes, _, length = state.shape
        count //= mesh.shape["parts"]
        params_here = tangents.shape[0] // (mesh.shape["parts"] * mesh.shape["field"])
        fits = (
            n & (n - 1) == 0
            and mesh.shape["field"] == 2
            and count * DEPTH == WIDE
            and others[-1].shape[0] == count
            and params_here * 2 == count
            and planes == mesh.shape["slab"]
            and n * LANES == length == state.shape[2]
            and length % WIDE == 0
        )
        local = functools.partial(pipelined, n) if fits else plain
        call = jax.shard_map(local, mesh=mesh, in_specs=in_specs, out_specs=out_specs, check_vma=False)
        return call(state, tangents, *others)

    return step
```

```python
import functools

import jax
import jax.numpy as jnp
from jax import lax
from jax.experimental import pallas as pl
from jax.experimental.pallas import tpu as pltpu
from jax.sharding import PartitionSpec as P


highest = lax.Precision.HIGHEST
time_step = 0.4
f32 = jnp.float32
bf16 = jnp.bfloat16
LANES = 128
WIDE = 2 * LANES
DEPTH = 32


def spread(values, fields):
    return values.reshape(values.shape + (1,) * (fields.ndim - values.ndim))


def reaction(state, tangent, coef, rates, offset):
    state_float = state.astype(f32)
    argument = jnp.einsum("ps,s...->p...", rates, state_float, precision=highest)
    activity = jnp.tanh(argument)
    slopes = 1.0 - activity * activity
    state_rate = jnp.einsum("ps,p...->s...", coef, activity, precision=highest)
    tangent_float = tangent.astype(f32)
    mixing = jnp.einsum("pt,qt...->qp...", rates, tangent_float, precision=highest)
    number = tangent.shape[0]
    own_coef = lax.dynamic_slice_in_dim(coef, offset, number, 0)
    own_activity = lax.dynamic_slice_in_dim(activity, offset, number, 0)
    tangent_rate = jnp.einsum("ps,qp...->qs...", coef, slopes[None] * mixing, precision=highest)
    tangent_rate = tangent_rate + spread(own_coef, tangent) * own_activity[:, None]
    return (state_rate, tangent_rate)


def update(fields, rate, speeds, diffusivity, operators):
    derivative_op, diffusion_op, filter_op = operators
    slope_term = jnp.dot(fields, derivative_op, preferred_element_type=f32)
    curve_term = jnp.dot(fields, diffusion_op, preferred_element_type=f32)
    middle = fields.astype(f32) + time_step * (
        spread(diffusivity, fields) * curve_term - spread(speeds, fields) * slope_term + rate
    )
    middle = middle.astype(bf16)
    return jnp.dot(middle, filter_op, preferred_element_type=f32).astype(bf16)


def plain(state, tangents, d1, d2, filt, advect, diffuse, coef, rates):
    params_here = tangents.shape[0]
    state_count = state.shape[0]
    offset = lax.axis_index("field") * params_here
    operators = (d1, d2, filt)
    for direction in range(2):
        speeds = advect[direction]
        state_rate, tangent_rate = reaction(state, tangents, coef, rates, offset)
        tangents = update(tangents, tangent_rate, speeds[None, :], diffuse[None, :], operators)
        outgoing = update(state, state_rate, speeds, diffuse, operators)
        merged = tangents.reshape((params_here * state_count,) + tangents.shape[2:])
        arrived = lax.all_to_all(outgoing, "pencil", split_axis=3, concat_axis=2, tiled=True)
        merged = lax.all_to_all(merged, "pencil", split_axis=3, concat_axis=2, tiled=True)
        state = jnp.swapaxes(arrived, 2, 3)
        merged = jnp.swapaxes(merged, 2, 3)
        tangents = merged.reshape((params_here, state_count) + merged.shape[1:])
    return (state, tangents)


def aligned(index, size):
    return pl.ds(pl.multiple_of(index * size, size), size)


def fill_mixer(entry, high, low):
    rows, columns = high.shape
    lane = lax.broadcasted_iota(jnp.int32, (8, columns), 1)
    row = lax.broadcasted_iota(jnp.int32, (8, columns), 0)
    group = lane // DEPTH
    within = lane - group * DEPTH
    for a in range(rows // DEPTH):
        values = jnp.zeros((8, columns), f32)
        for b in range(columns // DEPTH):
            values = jnp.where(group == b, entry(a, b), values)
        pieces = [jnp.where(within == row + 8 * k, values, 0.0) for k in range(DEPTH // 8)]
        block = jnp.concatenate(pieces, axis=0)
        rounded = block.astype(bf16)
        high[a * DEPTH : (a + 1) * DEPTH, :] = rounded
        low[a * DEPTH : (a + 1) * DEPTH, :] = (block - rounded.astype(f32)).astype(bf16)


def mixed(mixer, fields):
    high, low = mixer
    return jnp.dot(high[...], fields, preferred_element_type=f32) + jnp.dot(
        low[...], fields, preferred_element_type=f32
    )


def mixed_float(mixer, values):
    rounded = values.astype(bf16)
    left = (values - rounded.astype(f32)).astype(bf16)
    return mixed(mixer, rounded) + jnp.dot(mixer[0][...], left, preferred_element_type=f32)


def weighted(coef, s, channels):
    total = None
    for p in range(coef.shape[0]):
        term = coef[p, s] * channels[p * DEPTH : (p + 1) * DEPTH]
        total = term if total is None else total + term
    return total


def tangent_scaled(activity, mixing, own):
    scaled = (1.0 - activity * activity) * mixing
    group = lax.broadcasted_iota(jnp.int32, activity.shape, 0) // DEPTH
    return scaled + jnp.where(group == own, activity, 0.0)


def advance(v, curve, slope, rate, diffusivity, speed):
    return (v.astype(f32) + time_step * (diffusivity * curve - speed * slope + rate)).astype(bf16)


def x_state_kernel(n, *refs):
    far, outs, near, rest = refs[:8], refs[8 : 8 + n], refs[8 + n : 16 + n], refs[16 + n :]
    rates, coef, advect, diffuse, state, d1, d2, filt = near
    filt_own, rates_high, rates_low, rate, middle, ready, sems, out_sems = rest
    copies = [pltpu.make_async_copy(far[i], near[i], sems.at[i]) for i in range(8)]
    for copy in copies:
        copy.start()
    me, half = lax.axis_index("pencil"), lax.axis_index("field")
    count, _, rows, length = state.shape
    fields = outs[0].shape[0]
    size = length // n
    first = half * fields
    for copy in copies[:4]:
        copy.wait()
    fill_mixer(lambda a, b: rates[a, b], rates_high, rates_low)
    copies[4].wait()
    for j in range(rows // DEPTH):
        down = slice(j * DEPTH, (j + 1) * DEPTH)
        for c in range(length // WIDE):
            across = slice(c * WIDE, (c + 1) * WIDE)
            u = state[:, 0, down, across].reshape(count * DEPTH, WIDE)
            activity = jnp.tanh(mixed((rates_high, rates_low), u))
            for s in range(fields):
                at = slice(s * rows + j * DEPTH, s * rows + (j + 1) * DEPTH)
                rate[at, across] = weighted(coef, first + s, activity)
    own = state[pl.ds(first, fields), 0].reshape(fields * rows, length)
    copies[5].wait()
    copies[6].wait()
    for c in range(length // WIDE):
        across = slice(c * WIDE, (c + 1) * WIDE)
        slope = jnp.dot(own, d1[:, across], preferred_element_type=f32)
        curve = jnp.dot(own, d2[:, across], preferred_element_type=f32)
        for s in range(fields):
            at = slice(s * rows, (s + 1) * rows)
            middle[at, across] = advance(
                own[at, across], curve[at], slope[at], rate[at, across], diffuse[first + s], advect[0, first + s]
            )
    copies[7].wait()
    for r in range(n):
        filt_own[:, r * size : (r + 1) * size] = filt[:, aligned(me ^ r, size)]
    sends = []
    for c in reversed(range(length // WIDE)):
        across = slice(c * WIDE, (c + 1) * WIDE)
        result = jnp.dot(middle[...], filt_own[:, across], preferred_element_type=f32).astype(bf16)
        for k in range(WIDE // size):
            r = c * (WIDE // size) + k
            ready[r] = result[:, k * size : (k + 1) * size].reshape(fields, rows, size)
            sends.append(pltpu.make_async_copy(ready.at[r], outs[r], out_sems.at[r]))
            sends[-1].start()
    for send in sends:
        send.wait()


def x_kernel(n, q, params_here, rates, coef, advect, diffuse, state, tangent, d1, d2, filt, *rest):
    outs, rest = rest[:n], rest[n:]
    filt_own, rates_high, rates_low, middle = rest
    me, half = lax.axis_index("pencil"), lax.axis_index("field")
    count, rows, length = state.shape
    size = length // n

    @pl.when(pl.program_id(0) == 0)
    def _():
        fill_mixer(lambda a, b: rates[a, b], rates_high, rates_low)
        for r in range(n):
            filt_own[:, r * size : (r + 1) * size] = filt[:, aligned(me ^ r, size)]

    own = tangent[...].reshape(count * rows, length)
    for c in range(length // WIDE):
        across = slice(c * WIDE, (c + 1) * WIDE)
        u = state[:, :, across].reshape(count * rows, WIDE)
        activity = jnp.tanh(mixed((rates_high, rates_low), u))
        mixing = mixed((rates_high, rates_low), own[:, across])
        scaled = tangent_scaled(activity, mixing, half * params_here + q)
        slope = jnp.dot(own, d1[:, across], preferred_element_type=f32)
        curve = jnp.dot(own, d2[:, across], preferred_element_type=f32)
        for s in range(count):
            at = slice(s * rows, (s + 1) * rows)
            rate = weighted(coef, s, scaled)
            middle[at, across] = advance(
                own[at, across], curve[at], slope[at], rate, diffuse[s], advect[0, s]
            )
    result = jnp.dot(middle[...], filt_own[...], preferred_element_type=f32).astype(bf16)
    for r in range(n):
        outs[r][...] = result[:, r * size : (r + 1) * size].reshape(count, rows, size)


def y_kernel(n, q, params_here, rates, coef, advect, diffuse, *rest):
    own, rest = rest[:n], rest[n:]
    other, rest = rest[:n], rest[n:]
    if q is None:
        arrived = own
    else:
        arrived, rest = rest[:n], rest[n:]
    d1t, d2t, filtt = rest[:3]
    outs, rest = rest[3 : 3 + n], rest[3 + n :]
    filt_own, v_full, rate_full, state_high, state_low, coef_high, coef_low = rest[:7]
    me, half = lax.axis_index("pencil"), lax.axis_index("field")
    here = own[0].shape[0]
    count = rates.shape[1]
    size = own[0].shape[1]
    fields = outs[0].shape[0]
    first = half * here if q is None else 0

    fill_mixer(lambda a, b: rates[a, lax.rem(half * here + b, count)], state_high, state_low)
    fill_mixer(lambda a, b: coef[b, first + a], coef_high, coef_low)
    if q is not None:
        rates_high, rates_low = rest[7:]
        fill_mixer(lambda a, b: rates[a, b], rates_high, rates_low)

    def tile(refs, down):
        return jnp.concatenate([ref[:, down, :].reshape(ref.shape[0] * DEPTH, size) for ref in refs], axis=0)

    def pair(refs, j):
        starts = [(2 * j + k) * DEPTH for k in range(2)]
        return jnp.concatenate([tile(refs, pl.ds(pl.multiple_of(at, DEPTH), DEPTH)) for at in starts], axis=1)

    for r in range(n):
        filt_own[r * size : (r + 1) * size, :] = filtt[aligned(me ^ r, size), :]
        for s in range(fields):
            v_full[aligned(me ^ r, size), s * size : (s + 1) * size] = arrived[r][s]

        def rate_block(j, carry, r=r):
            activity = jnp.tanh(mixed((state_high, state_low), pair((own[r], other[r]), j)))
            if q is None:
                scaled = activity
            else:
                mixing = mixed((rates_high, rates_low), pair((arrived[r],), j))
                scaled = tangent_scaled(activity, mixing, half * params_here + q)
            rate = mixed_float((coef_high, coef_low), scaled)
            for k in range(2):
                down = pl.ds(pl.multiple_of((me ^ r) * size + (2 * j + k) * DEPTH, DEPTH), DEPTH)
                for s in range(fields):
                    rate_full[down, s * size : (s + 1) * size] = rate[
                        s * DEPTH : (s + 1) * DEPTH, k * size : (k + 1) * size
                    ]
            return carry

        lax.fori_loop(0, size // (2 * DEPTH), rate_block, 0)

    def two_fields(f, carry):
        v = v_full[:, aligned(f, 2 * size)]
        slope = jnp.dot(d1t[...], v, preferred_element_type=f32)
        curve = jnp.dot(d2t[...], v, preferred_element_type=f32)
        columns = []
        for k in range(2):
            s = 2 * f + k
            across = slice(k * size, (k + 1) * size)
            columns.append(
                advance(
                    v[:, across],
                    curve[:, across],
                    slope[:, across],
                    rate_full[:, aligned(s, size)],
                    diffuse[first + s],
                    advect[1, first + s],
                )
            )
        middle = jnp.concatenate(columns, axis=1)
        result = jnp.dot(filt_own[...], middle, preferred_element_type=f32).astype(bf16)
        for r in range(n):
            for k in range(2):
                outs[r][2 * f + k] = result[r * size : (r + 1) * size, k * size : (k + 1) * size]
        return carry

    lax.fori_loop(0, fields // 2, two_fields, 0)


def place_kernel(n, q, *rest):
    out, sems = rest[-2:]
    me, half = lax.axis_index("pencil"), lax.axis_index("field")
    groups = 2 if q is None else 1
    copies = []
    for g in range(groups):
        for r in range(n):
            slot = rest[g * n + r]
            here, _, size = slot.shape
            across = aligned(me ^ r, size)
            if q is None:
                target = out.at[aligned(half if g == 0 else 1 - half, here), 0, :, across]
            else:
                target = out.at[q, :, 0, :, across]
            copies.append(pltpu.make_async_copy(slot, target, sems.at[g * n + r]))
    for copy in copies:
        copy.start()
    for copy in copies:
        copy.wait()


SMEM = pl.BlockSpec(memory_space=pltpu.SMEM)
VMEM = pl.BlockSpec(memory_space=pltpu.VMEM)
HBM = pl.BlockSpec(memory_space=pl.ANY)
GRANT = pltpu.CompilerParams(vmem_limit_bytes=32 * 1024 * 1024)


def cost(flops, moved):
    return pl.CostEstimate(flops=flops, bytes_accessed=moved, transcendentals=0)


def mixers(fields, count):
    return [pltpu.VMEM((fields * DEPTH, count * DEPTH), bf16)] * 2


def x_state_call(n, scalars, state, d1, d2, filt, here):
    count, _, deep, length = state.shape
    square = pltpu.VMEM((length, length), bf16)
    return pl.pallas_call(
        functools.partial(x_state_kernel, n),
        out_shape=[jax.ShapeDtypeStruct((here, deep, length // n), bf16)] * n,
        in_specs=[HBM] * 8,
        out_specs=[HBM] * n,
        scratch_shapes=[pltpu.SMEM(scalar.shape, f32) for scalar in scalars]
        + [pltpu.VMEM(state.shape, bf16), square, square, square, square]
        + mixers(count, count)
        + [
            pltpu.VMEM((here * deep, length), f32),
            pltpu.VMEM((here * deep, length), bf16),
            pltpu.VMEM((n, here, deep, length // n), bf16),
            pltpu.SemaphoreType.DMA((8,)),
            pltpu.SemaphoreType.DMA((n,)),
        ],
        cost_estimate=cost(6 * here * deep * length * length, 4 * here * deep * length),
        name="x_state",
    )(*scalars, state, d1, d2, filt)


def x_call(n, q, scalars, state, tangents, d1, d2, filt):
    params_here, count, _, deep, length = tangents.shape
    size = length // n
    whole = pl.BlockSpec((length, length), lambda i: (0, 0))
    return pl.pallas_call(
        functools.partial(x_kernel, n, q, params_here),
        grid=(deep // DEPTH,),
        out_shape=[jax.ShapeDtypeStruct((count, deep, size), bf16)] * n,
        in_specs=[SMEM] * 4
        + [
            pl.BlockSpec((count, None, DEPTH, length), lambda i: (0, 0, i, 0)),
            pl.BlockSpec((None, count, None, DEPTH, length), lambda i: (q, 0, 0, i, 0)),
        ]
        + [whole] * 3,
        out_specs=[pl.BlockSpec((count, DEPTH, size), lambda i: (0, i, 0))] * n,
        scratch_shapes=[pltpu.VMEM((length, length), bf16)]
        + mixers(count, count)
        + [pltpu.VMEM((count * DEPTH, length), bf16)],
        cost_estimate=cost(6 * count * deep * length * length, 4 * count * deep * length),
    )(*scalars, state, tangents, d1, d2, filt)


def y_call(n, q, params_here, scalars, own, other, arrived, turned):
    here, deep, size = own[0].shape
    count = scalars[0].shape[1]
    length = deep * n
    fields = here if q is None else count
    arrays = list(own) + list(other) + list(arrived or ())
    return pl.pallas_call(
        functools.partial(y_kernel, n, q, params_here),
        out_shape=[jax.ShapeDtypeStruct((fields, deep, size), bf16)] * n,
        in_specs=[SMEM] * 4 + [VMEM] * (len(arrays) + 3),
        out_specs=[VMEM] * n,
        scratch_shapes=[
            pltpu.VMEM((length, length), bf16),
            pltpu.VMEM((length, fields * size), bf16),
            pltpu.VMEM((length, fields * size), f32),
        ]
        + mixers(count, count)
        + mixers(fields, count)
        + ([] if q is None else mixers(count, count)),
        compiler_params=GRANT,
        cost_estimate=cost(6 * fields * deep * length * length, 4 * fields * deep * length),
    )(*scalars, *arrays, *turned)


def place_state(n, shape, own, other):
    return pl.pallas_call(
        functools.partial(place_kernel, n, None),
        out_shape=jax.ShapeDtypeStruct(shape, bf16),
        in_specs=[VMEM] * (2 * n),
        out_specs=HBM,
        scratch_shapes=[pltpu.SemaphoreType.DMA((2 * n,))],
        compiler_params=GRANT,
        name="place_state",
    )(*own, *other)


def place_tangent(n, q, shape, slots, buffer):
    earlier = [] if buffer is None else [buffer]
    return pl.pallas_call(
        functools.partial(place_kernel, n, q),
        out_shape=jax.ShapeDtypeStruct(shape, bf16),
        in_specs=[VMEM] * n + [HBM] * len(earlier),
        out_specs=HBM,
        scratch_shapes=[pltpu.SemaphoreType.DMA((n,))],
        input_output_aliases={n: 0} if earlier else {},
        compiler_params=GRANT,
    )(*slots, *earlier)


def exchange(n, slots):
    order = list(range(n // 2, n)) + list(range(1, n // 2))
    arrived = {r: lax.ppermute(slots[r], "pencil", [(i, i ^ r) for i in range(n)]) for r in order}
    return [slots[0]] + [arrived[r] for r in range(1, n)]


def swap(slots):
    return [lax.ppermute(slot, "field", [(0, 1), (1, 0)]) for slot in slots]


def pipelined(n, state, tangents, d1, d2, filt, advect, diffuse, coef, rates):
    params = range(tangents.shape[0])
    here = state.shape[0] // 2
    scalars = (rates, coef, advect, diffuse)

    def forth(q):
        if q is None:
            return x_state_call(n, scalars, state, d1, d2, filt, here)
        return x_call(n, q, scalars, state, tangents, d1, d2, filt)

    own = exchange(n, forth(None))
    sent = [exchange(n, forth(q)) for q in params]
    turned = (d1.T, d2.T, filt.T)
    other = swap(own)

    def turn(q):
        return y_call(n, q, len(params), scalars, own, other, None if q is None else sent[q], turned)

    mine = exchange(n, turn(None))
    theirs = swap(mine)
    buffer = None
    for q in params:
        back = exchange(n, turn(q))
        buffer = place_tangent(n, q, tangents.shape, back, buffer)
    return (place_state(n, state.shape, mine, theirs), buffer)


def solution(mesh):
    in_specs = (
        P("parts", "slab", "pencil", None),
        P(("parts", "field"), None, "slab", "pencil", None),
        P(),
        P(),
        P(),
        P(),
        P(),
        P(),
        P(),
    )
    out_specs = (
        P("parts", "slab", "pencil", None),
        P(("parts", "field"), None, "slab", "pencil", None),
    )
    n = mesh.shape["pencil"]

    def step(state, tangents, *others):
        count, planes, _, length = state.shape
        count //= mesh.shape["parts"]
        params_here = tangents.shape[0] // (mesh.shape["parts"] * mesh.shape["field"])
        fits = (
            n & (n - 1) == 0
            and mesh.shape["field"] == 2
            and count * DEPTH == WIDE
            and others[-1].shape[0] == count
            and params_here * 2 == count
            and planes == mesh.shape["slab"]
            and n * LANES == length == state.shape[2]
            and length % WIDE == 0
        )
        local = functools.partial(pipelined, n) if fits else plain
        call = jax.shard_map(local, mesh=mesh, in_specs=in_specs, out_specs=out_specs, check_vma=False)
        return call(state, tangents, *others)

    return step
```

```python
import functools

import jax
import jax.numpy as jnp
from jax import lax
from jax.experimental import pallas as pl
from jax.experimental.pallas import tpu as pltpu
from jax.sharding import PartitionSpec as P


highest = lax.Precision.HIGHEST
time_step = 0.4
f32 = jnp.float32
bf16 = jnp.bfloat16
LANES = 128
WIDE = 2 * LANES
DEPTH = 32


def spread(values, fields):
    return values.reshape(values.shape + (1,) * (fields.ndim - values.ndim))


def reaction(state, tangent, coef, rates, offset):
    state_float = state.astype(f32)
    argument = jnp.einsum("ps,s...->p...", rates, state_float, precision=highest)
    activity = jnp.tanh(argument)
    slopes = 1.0 - activity * activity
    state_rate = jnp.einsum("ps,p...->s...", coef, activity, precision=highest)
    tangent_float = tangent.astype(f32)
    mixing = jnp.einsum("pt,qt...->qp...", rates, tangent_float, precision=highest)
    number = tangent.shape[0]
    own_coef = lax.dynamic_slice_in_dim(coef, offset, number, 0)
    own_activity = lax.dynamic_slice_in_dim(activity, offset, number, 0)
    tangent_rate = jnp.einsum("ps,qp...->qs...", coef, slopes[None] * mixing, precision=highest)
    tangent_rate = tangent_rate + spread(own_coef, tangent) * own_activity[:, None]
    return (state_rate, tangent_rate)


def update(fields, rate, speeds, diffusivity, operators):
    derivative_op, diffusion_op, filter_op = operators
    slope_term = jnp.dot(fields, derivative_op, preferred_element_type=f32)
    curve_term = jnp.dot(fields, diffusion_op, preferred_element_type=f32)
    middle = fields.astype(f32) + time_step * (
        spread(diffusivity, fields) * curve_term - spread(speeds, fields) * slope_term + rate
    )
    middle = middle.astype(bf16)
    return jnp.dot(middle, filter_op, preferred_element_type=f32).astype(bf16)


def plain(state, tangents, d1, d2, filt, advect, diffuse, coef, rates):
    params_here = tangents.shape[0]
    state_count = state.shape[0]
    offset = lax.axis_index("field") * params_here
    operators = (d1, d2, filt)
    for direction in range(2):
        speeds = advect[direction]
        state_rate, tangent_rate = reaction(state, tangents, coef, rates, offset)
        tangents = update(tangents, tangent_rate, speeds[None, :], diffuse[None, :], operators)
        outgoing = update(state, state_rate, speeds, diffuse, operators)
        merged = tangents.reshape((params_here * state_count,) + tangents.shape[2:])
        arrived = lax.all_to_all(outgoing, "pencil", split_axis=3, concat_axis=2, tiled=True)
        merged = lax.all_to_all(merged, "pencil", split_axis=3, concat_axis=2, tiled=True)
        state = jnp.swapaxes(arrived, 2, 3)
        merged = jnp.swapaxes(merged, 2, 3)
        tangents = merged.reshape((params_here, state_count) + merged.shape[1:])
    return (state, tangents)


def aligned(index, size):
    return pl.ds(pl.multiple_of(index * size, size), size)


def fill_mixer(entry, high, low):
    rows, columns = high.shape
    lane = lax.broadcasted_iota(jnp.int32, (8, columns), 1)
    row = lax.broadcasted_iota(jnp.int32, (8, columns), 0)
    group = lane // DEPTH
    within = lane - group * DEPTH
    for a in range(rows // DEPTH):
        values = jnp.zeros((8, columns), f32)
        for b in range(columns // DEPTH):
            values = jnp.where(group == b, entry(a, b), values)
        pieces = [jnp.where(within == row + 8 * k, values, 0.0) for k in range(DEPTH // 8)]
        block = jnp.concatenate(pieces, axis=0)
        rounded = block.astype(bf16)
        high[a * DEPTH : (a + 1) * DEPTH, :] = rounded
        low[a * DEPTH : (a + 1) * DEPTH, :] = (block - rounded.astype(f32)).astype(bf16)


def mixed(mixer, fields):
    high, low = mixer
    return jnp.dot(high[...], fields, preferred_element_type=f32) + jnp.dot(
        low[...], fields, preferred_element_type=f32
    )


def weighted(coef, s, channels):
    total = None
    for p in range(coef.shape[0]):
        term = coef[p, s] * channels[p * DEPTH : (p + 1) * DEPTH]
        total = term if total is None else total + term
    return total


def tangent_scaled(activity, mixing, own):
    scaled = (1.0 - activity * activity) * mixing
    group = lax.broadcasted_iota(jnp.int32, activity.shape, 0) // DEPTH
    return scaled + jnp.where(group == own, activity, 0.0)


def advance(v, curve, slope, rate, diffusivity, speed):
    return (v.astype(f32) + time_step * (diffusivity * curve - speed * slope + rate)).astype(bf16)


def x_state_kernel(n, *refs):
    far, outs, near, rest = refs[:8], refs[8 : 8 + n], refs[8 + n : 16 + n], refs[16 + n :]
    rates, coef, advect, diffuse, state, d1, d2, filt = near
    filt_own, rates_high, rates_low, rate, middle, ready, sems, out_sems = rest
    me, half = lax.axis_index("pencil"), lax.axis_index("field")
    fields, _, rows, length = state.shape
    size = length // n
    sources = list(far)
    sources[4] = far[4].at[:, :, aligned(half, rows), :]
    copies = [pltpu.make_async_copy(sources[i], near[i], sems.at[i]) for i in range(8)]
    for copy in copies:
        copy.start()
    for copy in copies[:4]:
        copy.wait()
    fill_mixer(lambda a, b: rates[a, b], rates_high, rates_low)
    copies[4].wait()
    own = state[:, 0].reshape(fields * rows, length)
    for c in range(length // WIDE):
        across = slice(c * WIDE, (c + 1) * WIDE)
        for j in range(rows // DEPTH):
            u = state[:, 0, j * DEPTH : (j + 1) * DEPTH, across].reshape(fields * DEPTH, WIDE)
            activity = jnp.tanh(mixed((rates_high, rates_low), u))
            for s in range(fields):
                at = slice(s * rows + j * DEPTH, s * rows + (j + 1) * DEPTH)
                rate[at, across] = weighted(coef, s, activity)
        if c == 0:
            for copy in copies[5:]:
                copy.wait()
        slope = jnp.dot(own, d1[:, across], preferred_element_type=f32)
        for s in range(fields):
            at = slice(s * rows, (s + 1) * rows)
            rate[at, across] = rate[at, across] - advect[0, s] * slope[at]
        curve = jnp.dot(own, d2[:, across], preferred_element_type=f32)
        for s in range(fields):
            at = slice(s * rows, (s + 1) * rows)
            moved = own[at, across].astype(f32) + time_step * (diffuse[s] * curve[at] + rate[at, across])
            middle[at, across] = moved.astype(bf16)
    for r in range(n):
        filt_own[:, r * size : (r + 1) * size] = filt[:, aligned(me ^ r, size)]
    sends = []
    for c in reversed(range(length // WIDE)):
        across = slice(c * WIDE, (c + 1) * WIDE)
        result = jnp.dot(middle[...], filt_own[:, across], preferred_element_type=f32).astype(bf16)
        for k in range(WIDE // size):
            r = c * (WIDE // size) + k
            ready[r] = result[:, k * size : (k + 1) * size].reshape(fields, rows, size)
            sends.append(pltpu.make_async_copy(ready.at[r], outs[r], out_sems.at[r]))
            sends[-1].start()
    for send in sends:
        send.wait()


def x_kernel(n, q, params_here, rates, coef, advect, diffuse, state, tangent, d1, d2, filt, *rest):
    outs, rest = rest[:n], rest[n:]
    filt_own, rates_high, rates_low, middle = rest
    me, half = lax.axis_index("pencil"), lax.axis_index("field")
    count, rows, length = state.shape
    size = length // n

    @pl.when(pl.program_id(0) == 0)
    def _():
        fill_mixer(lambda a, b: rates[a, b], rates_high, rates_low)
        for r in range(n):
            filt_own[:, r * size : (r + 1) * size] = filt[:, aligned(me ^ r, size)]

    own = tangent[...].reshape(count * rows, length)
    for c in range(length // WIDE):
        across = slice(c * WIDE, (c + 1) * WIDE)
        u = state[:, :, across].reshape(count * rows, WIDE)
        activity = jnp.tanh(mixed((rates_high, rates_low), u))
        mixing = mixed((rates_high, rates_low), own[:, across])
        scaled = tangent_scaled(activity, mixing, half * params_here + q)
        slope = jnp.dot(own, d1[:, across], preferred_element_type=f32)
        curve = jnp.dot(own, d2[:, across], preferred_element_type=f32)
        for s in range(count):
            at = slice(s * rows, (s + 1) * rows)
            rate = weighted(coef, s, scaled)
            middle[at, across] = advance(
                own[at, across], curve[at], slope[at], rate, diffuse[s], advect[0, s]
            )
    result = jnp.dot(middle[...], filt_own[...], preferred_element_type=f32).astype(bf16)
    for r in range(n):
        outs[r][...] = result[:, r * size : (r + 1) * size].reshape(count, rows, size)


def y_kernel(n, q, params_here, rates, coef, advect, diffuse, *rest):
    own, other, rest = rest[:n], rest[n : 2 * n], rest[2 * n :]
    if q is not None:
        arrived, rest = rest[:n], rest[n:]
    d1t, d2t, filtt = rest[:3]
    outs, rest = rest[3 : 3 + n], rest[3 + n :]
    filt_own, u_full, rate_full, rates_high, rates_low = rest[:5]
    v_full = u_full if q is None else rest[5]
    me, half = lax.axis_index("pencil"), lax.axis_index("field")
    count, rows, size = own[0].shape
    fields = outs[0].shape[0]
    first = half * fields if q is None else 0
    fill_mixer(lambda a, b: rates[a, b], rates_high, rates_low)

    for r in range(n):
        filt_own[r * size : (r + 1) * size, :] = filtt[aligned(me ^ r, size), :]
        for s in range(count):
            across = slice(s * size, (s + 1) * size)
            u_full[aligned(2 * (me ^ r) + half, rows), across] = own[r][s]
            u_full[aligned(2 * (me ^ r) + 1 - half, rows), across] = other[r][s]
            if q is not None:
                v_full[aligned(me ^ r, size), across] = arrived[r][s]

    def pair(full, block):
        tiles = []
        for k in range(2):
            down = aligned(2 * block + k, DEPTH)
            tiles.append(
                jnp.concatenate([full[down, s * size : (s + 1) * size] for s in range(count)], axis=0)
            )
        return jnp.concatenate(tiles, axis=1)

    def rate_block(block, carry):
        scaled = jnp.tanh(mixed((rates_high, rates_low), pair(u_full, block)))
        if q is not None:
            mixing = mixed((rates_high, rates_low), pair(v_full, block))
            scaled = tangent_scaled(scaled, mixing, half * params_here + q)
        for s in range(fields):
            rate = weighted(coef, first + s, scaled)
            for k in range(2):
                rate_full[aligned(2 * block + k, DEPTH), s * size : (s + 1) * size] = rate[
                    :, k * size : (k + 1) * size
                ]
        return carry

    lax.fori_loop(0, n * size // (2 * DEPTH), rate_block, 0)

    def two_fields(f, carry):
        v = v_full[:, aligned(first // 2 + f, 2 * size)]
        slope = jnp.dot(d1t[...], v, preferred_element_type=f32)
        curve = jnp.dot(d2t[...], v, preferred_element_type=f32)
        columns = []
        for k in range(2):
            s = 2 * f + k
            across = slice(k * size, (k + 1) * size)
            columns.append(
                advance(
                    v[:, across],
                    curve[:, across],
                    slope[:, across],
                    rate_full[:, aligned(s, size)],
                    diffuse[first + s],
                    advect[1, first + s],
                )
            )
        middle = jnp.concatenate(columns, axis=1)
        result = jnp.dot(filt_own[...], middle, preferred_element_type=f32).astype(bf16)
        for r in range(n):
            for k in range(2):
                outs[r][2 * f + k] = result[r * size : (r + 1) * size, k * size : (k + 1) * size]
        return carry

    lax.fori_loop(0, fields // 2, two_fields, 0)


def place_kernel(n, q, some, *rest):
    out, sems = rest[-2:]
    me, half = lax.axis_index("pencil"), lax.axis_index("field")
    groups = 2 if q is None else 1
    copies = []
    for g in range(groups):
        for i, r in enumerate(some):
            slot = rest[g * n + i]
            here, _, size = slot.shape
            across = aligned(me ^ r, size)
            if q is None:
                target = out.at[aligned(half if g == 0 else 1 - half, here), 0, :, across]
            else:
                target = out.at[q, :, 0, :, across]
            copies.append(pltpu.make_async_copy(slot, target, sems.at[g * n + i]))
    for copy in copies:
        copy.start()
    for copy in copies:
        copy.wait()


SMEM = pl.BlockSpec(memory_space=pltpu.SMEM)
VMEM = pl.BlockSpec(memory_space=pltpu.VMEM)
HBM = pl.BlockSpec(memory_space=pl.ANY)
GRANT = pltpu.CompilerParams(vmem_limit_bytes=32 * 1024 * 1024)


def cost(flops, moved):
    return pl.CostEstimate(flops=flops, bytes_accessed=moved, transcendentals=0)


def mixers(fields, count):
    return [pltpu.VMEM((fields * DEPTH, count * DEPTH), bf16)] * 2


def x_state_call(n, scalars, state, d1, d2, filt):
    count, _, deep, length = state.shape
    rows = deep // 2
    square = pltpu.VMEM((length, length), bf16)
    return pl.pallas_call(
        functools.partial(x_state_kernel, n),
        out_shape=[jax.ShapeDtypeStruct((count, rows, length // n), bf16)] * n,
        in_specs=[HBM] * 8,
        out_specs=[HBM] * n,
        scratch_shapes=[pltpu.SMEM(scalar.shape, f32) for scalar in scalars]
        + [pltpu.VMEM((count, 1, rows, length), bf16), square, square, square, square]
        + mixers(count, count)
        + [
            pltpu.VMEM((count * rows, length), f32),
            pltpu.VMEM((count * rows, length), bf16),
            pltpu.VMEM((n, count, rows, length // n), bf16),
            pltpu.SemaphoreType.DMA((8,)),
            pltpu.SemaphoreType.DMA((n,)),
        ],
        cost_estimate=cost(6 * count * rows * length * length, 4 * count * rows * length),
        name="x_state",
    )(*scalars, state, d1, d2, filt)


def x_call(n, q, scalars, state, tangents, d1, d2, filt):
    params_here, count, _, deep, length = tangents.shape
    size = length // n
    whole = pl.BlockSpec((length, length), lambda i: (0, 0))
    return pl.pallas_call(
        functools.partial(x_kernel, n, q, params_here),
        grid=(deep // DEPTH,),
        out_shape=[jax.ShapeDtypeStruct((count, deep, size), bf16)] * n,
        in_specs=[SMEM] * 4
        + [
            pl.BlockSpec((count, None, DEPTH, length), lambda i: (0, 0, i, 0)),
            pl.BlockSpec((None, count, None, DEPTH, length), lambda i: (q, 0, 0, i, 0)),
        ]
        + [whole] * 3,
        out_specs=[pl.BlockSpec((count, DEPTH, size), lambda i: (0, i, 0))] * n,
        scratch_shapes=[pltpu.VMEM((length, length), bf16)]
        + mixers(count, count)
        + [pltpu.VMEM((count * DEPTH, length), bf16)],
        cost_estimate=cost(6 * count * deep * length * length, 4 * count * deep * length),
    )(*scalars, state, tangents, d1, d2, filt)


def y_call(n, q, params_here, scalars, own, other, arrived, turned):
    count, _, size = own[0].shape
    length = size * n
    fields = count // 2 if q is None else count
    arrays = list(own) + list(other) + list(arrived or ())
    full = pltpu.VMEM((length, count * size), bf16)
    return pl.pallas_call(
        functools.partial(y_kernel, n, q, params_here),
        out_shape=[jax.ShapeDtypeStruct((fields, size, size), bf16)] * n,
        in_specs=[SMEM] * 4 + [VMEM] * (len(arrays) + 3),
        out_specs=[VMEM] * n,
        scratch_shapes=[pltpu.VMEM((length, length), bf16), full, pltpu.VMEM((length, fields * size), f32)]
        + mixers(count, count)
        + ([] if q is None else [full]),
        compiler_params=GRANT,
        cost_estimate=cost(6 * fields * size * length * length, 4 * fields * size * length),
    )(*scalars, *arrays, *turned)


def place_state(n, shape, own, other):
    return pl.pallas_call(
        functools.partial(place_kernel, n, None, range(n)),
        out_shape=jax.ShapeDtypeStruct(shape, bf16),
        in_specs=[VMEM] * (2 * n),
        out_specs=HBM,
        scratch_shapes=[pltpu.SemaphoreType.DMA((2 * n,))],
        compiler_params=GRANT,
        name="place_state",
    )(*own, *other)


def place_tangent(n, q, some, shape, slots, buffer):
    slots = [slots[r] for r in some]
    earlier = [] if buffer is None else [buffer]
    return pl.pallas_call(
        functools.partial(place_kernel, n, q, some),
        out_shape=jax.ShapeDtypeStruct(shape, bf16),
        in_specs=[VMEM] * len(slots) + [HBM] * len(earlier),
        out_specs=HBM,
        scratch_shapes=[pltpu.SemaphoreType.DMA((len(slots),))],
        input_output_aliases={len(slots): 0} if earlier else {},
        compiler_params=GRANT,
    )(*slots, *earlier)


def exchange(n, slots):
    order = list(range(n // 2, n)) + list(range(1, n // 2))
    arrived = {}
    for r in order:
        arrived[r] = lax.ppermute(slots[r], "pencil", [(i, i ^ r) for i in range(n)])
    return [slots[0]] + [arrived[r] for r in range(1, n)]


def swap(slots):
    return [lax.ppermute(slot, "field", [(0, 1), (1, 0)]) for slot in slots]


def pipelined(n, state, tangents, d1, d2, filt, advect, diffuse, coef, rates):
    params = range(tangents.shape[0])
    scalars = (rates, coef, advect, diffuse)

    def forth(q):
        if q is None:
            return x_state_call(n, scalars, state, d1, d2, filt)
        return x_call(n, q, scalars, state, tangents, d1, d2, filt)

    own = exchange(n, forth(None))
    sent = [exchange(n, forth(q)) for q in params]
    turned = (d1.T, d2.T, filt.T)
    other = swap(own)

    def turn(q):
        return y_call(n, q, len(params), scalars, own, other, None if q is None else sent[q], turned)

    mine = exchange(n, turn(None))
    theirs = swap(mine)
    buffer = None
    for q in params:
        back = exchange(n, turn(q))
        early = range(n if q < params[-1] else n - 1)
        buffer = place_tangent(n, q, early, tangents.shape, back, buffer)
    buffer = place_tangent(n, q, range(n - 1, n), tangents.shape, back, buffer)
    return (place_state(n, state.shape, mine, theirs), buffer)


def solution(mesh):
    in_specs = (
        P("parts", "slab", "pencil", None),
        P(("parts", "field"), None, "slab", "pencil", None),
        P(),
        P(),
        P(),
        P(),
        P(),
        P(),
        P(),
    )
    out_specs = (
        P("parts", "slab", "pencil", None),
        P(("parts", "field"), None, "slab", "pencil", None),
    )
    n = mesh.shape["pencil"]

    def step(state, tangents, *others):
        count, planes, _, length = state.shape
        count //= mesh.shape["parts"]
        params_here = tangents.shape[0] // (mesh.shape["parts"] * mesh.shape["field"])
        fits = (
            n & (n - 1) == 0
            and mesh.shape["field"] == 2
            and count * DEPTH == WIDE
            and others[-1].shape[0] == count
            and params_here * 2 == count
            and planes == mesh.shape["slab"]
            and n * LANES == length == state.shape[2]
            and length % WIDE == 0
        )
        local = functools.partial(pipelined, n) if fits else plain
        call = jax.shard_map(local, mesh=mesh, in_specs=in_specs, out_specs=out_specs, check_vma=False)
        return call(state, tangents, *others)

    return step
```

```python
import functools

import jax
import jax.numpy as jnp
from jax import lax
from jax.experimental import pallas as pl
from jax.experimental.pallas import tpu as pltpu
from jax.sharding import PartitionSpec as P


highest = lax.Precision.HIGHEST
time_step = 0.4
f32 = jnp.float32
bf16 = jnp.bfloat16
LANES = 128
WIDE = 2 * LANES
DEPTH = 32
PARTS = 1


def spread(values, fields):
    return values.reshape(values.shape + (1,) * (fields.ndim - values.ndim))


def reaction(state, tangent, coef, rates, offset):
    state_float = state.astype(f32)
    argument = jnp.einsum("ps,s...->p...", rates, state_float, precision=highest)
    activity = jnp.tanh(argument)
    slopes = 1.0 - activity * activity
    state_rate = jnp.einsum("ps,p...->s...", coef, activity, precision=highest)
    tangent_float = tangent.astype(f32)
    mixing = jnp.einsum("pt,qt...->qp...", rates, tangent_float, precision=highest)
    number = tangent.shape[0]
    own_coef = lax.dynamic_slice_in_dim(coef, offset, number, 0)
    own_activity = lax.dynamic_slice_in_dim(activity, offset, number, 0)
    tangent_rate = jnp.einsum("ps,qp...->qs...", coef, slopes[None] * mixing, precision=highest)
    tangent_rate = tangent_rate + spread(own_coef, tangent) * own_activity[:, None]
    return (state_rate, tangent_rate)


def update(fields, rate, speeds, diffusivity, operators):
    derivative_op, diffusion_op, filter_op = operators
    slope_term = jnp.dot(fields, derivative_op, preferred_element_type=f32)
    curve_term = jnp.dot(fields, diffusion_op, preferred_element_type=f32)
    middle = fields.astype(f32) + time_step * (
        spread(diffusivity, fields) * curve_term - spread(speeds, fields) * slope_term + rate
    )
    middle = middle.astype(bf16)
    return jnp.dot(middle, filter_op, preferred_element_type=f32).astype(bf16)


def plain(state, tangents, d1, d2, filt, advect, diffuse, coef, rates):
    params_here = tangents.shape[0]
    state_count = state.shape[0]
    offset = lax.axis_index("field") * params_here
    operators = (d1, d2, filt)
    for direction in range(2):
        speeds = advect[direction]
        state_rate, tangent_rate = reaction(state, tangents, coef, rates, offset)
        tangents = update(tangents, tangent_rate, speeds[None, :], diffuse[None, :], operators)
        outgoing = update(state, state_rate, speeds, diffuse, operators)
        merged = tangents.reshape((params_here * state_count,) + tangents.shape[2:])
        arrived = lax.all_to_all(outgoing, "pencil", split_axis=3, concat_axis=2, tiled=True)
        merged = lax.all_to_all(merged, "pencil", split_axis=3, concat_axis=2, tiled=True)
        state = jnp.swapaxes(arrived, 2, 3)
        merged = jnp.swapaxes(merged, 2, 3)
        tangents = merged.reshape((params_here, state_count) + merged.shape[1:])
    return (state, tangents)


def aligned(index, size):
    return pl.ds(pl.multiple_of(index * size, size), size)


def fill_mixer(entry, high, low):
    rows, columns = high.shape
    lane = lax.broadcasted_iota(jnp.int32, (8, columns), 1)
    row = lax.broadcasted_iota(jnp.int32, (8, columns), 0)
    group = lane // DEPTH
    within = lane - group * DEPTH
    for a in range(rows // DEPTH):
        values = jnp.zeros((8, columns), f32)
        for b in range(columns // DEPTH):
            values = jnp.where(group == b, entry(a, b), values)
        pieces = [jnp.where(within == row + 8 * k, values, 0.0) for k in range(DEPTH // 8)]
        block = jnp.concatenate(pieces, axis=0)
        rounded = block.astype(bf16)
        high[a * DEPTH : (a + 1) * DEPTH, :] = rounded
        low[a * DEPTH : (a + 1) * DEPTH, :] = (block - rounded.astype(f32)).astype(bf16)


def mixed(mixer, fields):
    high, low = mixer
    return jnp.dot(high[...], fields, preferred_element_type=f32) + jnp.dot(
        low[...], fields, preferred_element_type=f32
    )


def weighted(coef, s, channels):
    total = None
    for p in range(coef.shape[0]):
        term = coef[p, s] * channels[p * DEPTH : (p + 1) * DEPTH]
        total = term if total is None else total + term
    return total


def tangent_scaled(activity, mixing, own):
    scaled = (1.0 - activity * activity) * mixing
    group = lax.broadcasted_iota(jnp.int32, activity.shape, 0) // DEPTH
    return scaled + jnp.where(group == own, activity, 0.0)


def advance(v, curve, slope, rate, diffusivity, speed):
    return (v.astype(f32) + time_step * (diffusivity * curve - speed * slope + rate)).astype(bf16)


def x_state_kernel(n, part, *refs):
    kept = n // 2
    far, outs, near, rest = refs[:8], refs[8 : 9 + kept], refs[9 + kept : 17 + kept], refs[17 + kept :]
    rates, coef, advect, diffuse, state, d1, d2, filt = near
    filt_own, rates_high, rates_low, rate, middle, ready, sems, out_sems = rest
    me, half = lax.axis_index("pencil"), lax.axis_index("field")
    fields, _, rows, length = state.shape
    size = length // n
    sources = list(far)
    sources[4] = far[4].at[:, :, aligned(PARTS * half + part, rows), :]
    copies = [pltpu.make_async_copy(sources[i], near[i], sems.at[i]) for i in range(8)]
    for copy in copies:
        copy.start()
    for copy in copies[:4]:
        copy.wait()
    fill_mixer(lambda a, b: rates[a, b], rates_high, rates_low)
    copies[4].wait()
    own = state[:, 0].reshape(fields * rows, length)
    for c in range(length // WIDE):
        across = slice(c * WIDE, (c + 1) * WIDE)
        for j in range(rows // DEPTH):
            u = state[:, 0, j * DEPTH : (j + 1) * DEPTH, across].reshape(fields * DEPTH, WIDE)
            activity = jnp.tanh(mixed((rates_high, rates_low), u))
            for s in range(fields):
                at = slice(s * rows + j * DEPTH, s * rows + (j + 1) * DEPTH)
                rate[at, across] = weighted(coef, s, activity)
        if c == 0:
            for copy in copies[5:]:
                copy.wait()
        slope = jnp.dot(own, d1[:, across], preferred_element_type=f32)
        for s in range(fields):
            at = slice(s * rows, (s + 1) * rows)
            rate[at, across] = rate[at, across] - advect[0, s] * slope[at]
        curve = jnp.dot(own, d2[:, across], preferred_element_type=f32)
        for s in range(fields):
            at = slice(s * rows, (s + 1) * rows)
            moved = own[at, across].astype(f32) + time_step * (diffuse[s] * curve[at] + rate[at, across])
            middle[at, across] = moved.astype(bf16)
    for r in range(n):
        filt_own[:, r * size : (r + 1) * size] = filt[:, aligned(me ^ r, size)]
    for c in reversed(range(length // WIDE)):
        across = slice(c * WIDE, (c + 1) * WIDE)
        result = jnp.dot(middle[...], filt_own[:, across], preferred_element_type=f32).astype(bf16)
        for k in range(WIDE // size):
            r = c * (WIDE // size) + k
            ready[r] = result[:, k * size : (k + 1) * size].reshape(fields, rows, size)
        if c * (WIDE // size) == kept:
            sends = [pltpu.make_async_copy(ready.at[pl.ds(kept, n - kept)], outs[kept], out_sems.at[kept])]
            sends[0].start()
    for r in range(kept):
        sends.append(pltpu.make_async_copy(ready.at[r], outs[r], out_sems.at[r]))
        sends[-1].start()
    for send in sends:
        send.wait()


def x_kernel(n, q, params_here, rates, coef, advect, diffuse, state, tangent, d1, d2, filt, *rest):
    outs, rest = rest[:n], rest[n:]
    filt_own, rates_high, rates_low, middle = rest
    me, half = lax.axis_index("pencil"), lax.axis_index("field")
    count, rows, length = state.shape
    size = length // n

    @pl.when(pl.program_id(0) == 0)
    def _():
        fill_mixer(lambda a, b: rates[a, b], rates_high, rates_low)
        for r in range(n):
            filt_own[:, r * size : (r + 1) * size] = filt[:, aligned(me ^ r, size)]

    own = tangent[...].reshape(count * rows, length)
    for c in range(length // WIDE):
        across = slice(c * WIDE, (c + 1) * WIDE)
        u = state[:, :, across].reshape(count * rows, WIDE)
        activity = jnp.tanh(mixed((rates_high, rates_low), u))
        mixing = mixed((rates_high, rates_low), own[:, across])
        scaled = tangent_scaled(activity, mixing, half * params_here + q)
        slope = jnp.dot(own, d1[:, across], preferred_element_type=f32)
        curve = jnp.dot(own, d2[:, across], preferred_element_type=f32)
        for s in range(count):
            at = slice(s * rows, (s + 1) * rows)
            rate = weighted(coef, s, scaled)
            middle[at, across] = advance(
                own[at, across], curve[at], slope[at], rate, diffuse[s], advect[0, s]
            )
    result = jnp.dot(middle[...], filt_own[...], preferred_element_type=f32).astype(bf16)
    for r in range(n):
        outs[r][...] = result[:, r * size : (r + 1) * size].reshape(count, rows, size)


def y_kernel(n, q, params_here, rates, coef, advect, diffuse, *rest):
    pieces = PARTS * n
    own, other, rest = rest[:pieces], rest[pieces : 2 * pieces], rest[2 * pieces :]
    if q is not None:
        arrived, rest = rest[:n], rest[n:]
    d1t, d2t, filtt = rest[:3]
    outs, rest = rest[3 : 3 + n], rest[3 + n :]
    filt_own, u_full, rate_full, rates_high, rates_low = rest[:5]
    v_full = u_full if q is None else rest[5]
    me, half = lax.axis_index("pencil"), lax.axis_index("field")
    count, rows, size = own[0].shape
    fields = outs[0].shape[0]
    first = half * fields if q is None else 0
    fill_mixer(lambda a, b: rates[a, b], rates_high, rates_low)

    for r in range(n):
        filt_own[r * size : (r + 1) * size, :] = filtt[aligned(me ^ r, size), :]
        for s in range(count):
            across = slice(s * size, (s + 1) * size)
            for part in range(PARTS):
                here, there = PARTS * half + part, PARTS * (1 - half) + part
                u_full[aligned(2 * PARTS * (me ^ r) + here, rows), across] = own[part * n + r][s]
                u_full[aligned(2 * PARTS * (me ^ r) + there, rows), across] = other[part * n + r][s]
            if q is not None:
                v_full[aligned(me ^ r, size), across] = arrived[r][s]

    def pair(full, block):
        tiles = []
        for k in range(2):
            down = aligned(2 * block + k, DEPTH)
            tiles.append(
                jnp.concatenate([full[down, s * size : (s + 1) * size] for s in range(count)], axis=0)
            )
        return jnp.concatenate(tiles, axis=1)

    def rate_block(block, carry):
        scaled = jnp.tanh(mixed((rates_high, rates_low), pair(u_full, block)))
        if q is not None:
            mixing = mixed((rates_high, rates_low), pair(v_full, block))
            scaled = tangent_scaled(scaled, mixing, half * params_here + q)
        for s in range(fields):
            rate = weighted(coef, first + s, scaled)
            for k in range(2):
                rate_full[aligned(2 * block + k, DEPTH), s * size : (s + 1) * size] = rate[
                    :, k * size : (k + 1) * size
                ]
        return carry

    lax.fori_loop(0, n * size // (2 * DEPTH), rate_block, 0)

    def two_fields(f, carry):
        v = v_full[:, aligned(first // 2 + f, 2 * size)]
        slope = jnp.dot(d1t[...], v, preferred_element_type=f32)
        curve = jnp.dot(d2t[...], v, preferred_element_type=f32)
        columns = []
        for k in range(2):
            s = 2 * f + k
            across = slice(k * size, (k + 1) * size)
            columns.append(
                advance(
                    v[:, across],
                    curve[:, across],
                    slope[:, across],
                    rate_full[:, aligned(s, size)],
                    diffuse[first + s],
                    advect[1, first + s],
                )
            )
        middle = jnp.concatenate(columns, axis=1)
        result = jnp.dot(filt_own[...], middle, preferred_element_type=f32).astype(bf16)
        for r in range(n):
            for k in range(2):
                outs[r][2 * f + k] = result[r * size : (r + 1) * size, k * size : (k + 1) * size]
        return carry

    lax.fori_loop(0, fields // 2, two_fields, 0)


def place_kernel(n, q, some, *rest):
    out, sems = rest[-2:]
    me, half = lax.axis_index("pencil"), lax.axis_index("field")
    groups = 2 if q is None else 1
    copies = []
    for g in range(groups):
        for i, r in enumerate(some):
            slot = rest[g * n + i]
            here, _, size = slot.shape
            across = aligned(me ^ r, size)
            if q is None:
                target = out.at[aligned(half if g == 0 else 1 - half, here), 0, :, across]
            else:
                target = out.at[q, :, 0, :, across]
            copies.append(pltpu.make_async_copy(slot, target, sems.at[g * n + i]))
    for copy in copies:
        copy.start()
    for copy in copies:
        copy.wait()


SMEM = pl.BlockSpec(memory_space=pltpu.SMEM)
VMEM = pl.BlockSpec(memory_space=pltpu.VMEM)
HBM = pl.BlockSpec(memory_space=pl.ANY)
GRANT = pltpu.CompilerParams(vmem_limit_bytes=32 * 1024 * 1024)


def cost(flops, moved):
    return pl.CostEstimate(flops=flops, bytes_accessed=moved, transcendentals=0)


def mixers(fields, count):
    return [pltpu.VMEM((fields * DEPTH, count * DEPTH), bf16)] * 2


def x_state_call(n, part, scalars, state, d1, d2, filt):
    count, _, deep, length = state.shape
    rows = deep // (2 * PARTS)
    kept = n // 2
    block = (count, rows, length // n)
    square = pltpu.VMEM((length, length), bf16)
    return pl.pallas_call(
        functools.partial(x_state_kernel, n, part),
        out_shape=[jax.ShapeDtypeStruct(block, bf16)] * kept
        + [jax.ShapeDtypeStruct((n - kept,) + block, bf16)],
        in_specs=[HBM] * 8,
        out_specs=[HBM] * (kept + 1),
        scratch_shapes=[pltpu.SMEM(scalar.shape, f32) for scalar in scalars]
        + [pltpu.VMEM((count, 1, rows, length), bf16), square, square, square, square]
        + mixers(count, count)
        + [
            pltpu.VMEM((count * rows, length), f32),
            pltpu.VMEM((count * rows, length), bf16),
            pltpu.VMEM((n, count, rows, length // n), bf16),
            pltpu.SemaphoreType.DMA((8,)),
            pltpu.SemaphoreType.DMA((kept + 1,)),
        ],
        cost_estimate=cost(6 * count * rows * length * length, 4 * count * rows * length),
    )(*scalars, state, d1, d2, filt)


def x_call(n, q, scalars, state, tangents, d1, d2, filt):
    params_here, count, _, deep, length = tangents.shape
    size = length // n
    whole = pl.BlockSpec((length, length), lambda i: (0, 0))
    return pl.pallas_call(
        functools.partial(x_kernel, n, q, params_here),
        grid=(deep // DEPTH,),
        out_shape=[jax.ShapeDtypeStruct((count, deep, size), bf16)] * n,
        in_specs=[SMEM] * 4
        + [
            pl.BlockSpec((count, None, DEPTH, length), lambda i: (0, 0, i, 0)),
            pl.BlockSpec((None, count, None, DEPTH, length), lambda i: (q, 0, 0, i, 0)),
        ]
        + [whole] * 3,
        out_specs=[pl.BlockSpec((count, DEPTH, size), lambda i: (0, i, 0))] * n,
        scratch_shapes=[pltpu.VMEM((length, length), bf16)]
        + mixers(count, count)
        + [pltpu.VMEM((count * DEPTH, length), bf16)],
        cost_estimate=cost(6 * count * deep * length * length, 4 * count * deep * length),
    )(*scalars, state, tangents, d1, d2, filt)


def y_call(n, q, params_here, scalars, own, other, arrived, turned):
    count, _, size = own[0].shape
    length = size * n
    fields = count // 2 if q is None else count
    arrays = list(own) + list(other) + list(arrived or ())
    full = pltpu.VMEM((length, count * size), bf16)
    return pl.pallas_call(
        functools.partial(y_kernel, n, q, params_here),
        out_shape=[jax.ShapeDtypeStruct((fields, size, size), bf16)] * n,
        in_specs=[SMEM] * 4 + [VMEM] * (len(arrays) + 3),
        out_specs=[VMEM] * n,
        scratch_shapes=[pltpu.VMEM((length, length), bf16), full, pltpu.VMEM((length, fields * size), f32)]
        + mixers(count, count)
        + ([] if q is None else [full]),
        compiler_params=GRANT,
        cost_estimate=cost(6 * fields * size * length * length, 4 * fields * size * length),
    )(*scalars, *arrays, *turned)


def place_state(n, shape, own, other):
    return pl.pallas_call(
        functools.partial(place_kernel, n, None, range(n)),
        out_shape=jax.ShapeDtypeStruct(shape, bf16),
        in_specs=[VMEM] * (2 * n),
        out_specs=HBM,
        scratch_shapes=[pltpu.SemaphoreType.DMA((2 * n,))],
        compiler_params=GRANT,
        name="place_state",
    )(*own, *other)


def place_tangent(n, q, some, shape, slots, buffer):
    slots = [slots[r] for r in some]
    earlier = [] if buffer is None else [buffer]
    return pl.pallas_call(
        functools.partial(place_kernel, n, q, some),
        out_shape=jax.ShapeDtypeStruct(shape, bf16),
        in_specs=[VMEM] * len(slots) + [HBM] * len(earlier),
        out_specs=HBM,
        scratch_shapes=[pltpu.SemaphoreType.DMA((len(slots),))],
        input_output_aliases={len(slots): 0} if earlier else {},
        compiler_params=GRANT,
    )(*slots, *earlier)


def exchange(n, slots):
    order = list(range(n // 2, n)) + list(range(1, n // 2))
    arrived = {}
    for r in order:
        arrived[r] = lax.ppermute(slots[r], "pencil", [(i, i ^ r) for i in range(n)])
    return [slots[0]] + [arrived[r] for r in range(1, n)]


def exchange_state(n, made):
    kept = n // 2
    landed = lax.ppermute(made[kept], "pencil", [(i, i ^ kept) for i in range(n)])
    slots = [made[0]] + [None] * (kept - 1) + [landed[0]] + [None] * (kept - 1)
    for r in range(1, kept):
        pairs = [(i, i ^ r) for i in range(n)]
        slots[r] = lax.ppermute(made[r], "pencil", pairs)
        slots[kept + r] = lax.ppermute(landed[r], "pencil", pairs)
    return slots


def swap(slots):
    return [lax.ppermute(slot, "field", [(0, 1), (1, 0)]) for slot in slots]


def pipelined(n, state, tangents, d1, d2, filt, advect, diffuse, coef, rates):
    params = range(tangents.shape[0])
    scalars = (rates, coef, advect, diffuse)

    def forth_state(part):
        return x_state_call(n, part, scalars, state, d1, d2, filt)

    def forth(q):
        return x_call(n, q, scalars, state, tangents, d1, d2, filt)

    own = []
    for part in range(PARTS):
        own += exchange_state(n, forth_state(part))
    sent = [exchange(n, forth(q)) for q in params]
    turned = (d1.T, d2.T, filt.T)
    other = swap(own)

    def turn(q):
        return y_call(n, q, len(params), scalars, own, other, None if q is None else sent[q], turned)

    mine = exchange(n, turn(None))
    theirs = swap(mine)
    buffer = None
    for q in params:
        back = exchange(n, turn(q))
        early = range(n if q < params[-1] else n - 1)
        buffer = place_tangent(n, q, early, tangents.shape, back, buffer)
    buffer = place_tangent(n, q, range(n - 1, n), tangents.shape, back, buffer)
    return (place_state(n, state.shape, mine, theirs), buffer)


def solution(mesh):
    in_specs = (
        P("parts", "slab", "pencil", None),
        P(("parts", "field"), None, "slab", "pencil", None),
        P(),
        P(),
        P(),
        P(),
        P(),
        P(),
        P(),
    )
    out_specs = (
        P("parts", "slab", "pencil", None),
        P(("parts", "field"), None, "slab", "pencil", None),
    )
    n = mesh.shape["pencil"]

    def step(state, tangents, *others):
        count, planes, _, length = state.shape
        count //= mesh.shape["parts"]
        params_here = tangents.shape[0] // (mesh.shape["parts"] * mesh.shape["field"])
        fits = (
            n & (n - 1) == 0
            and mesh.shape["field"] == 2
            and count * DEPTH == WIDE
            and others[-1].shape[0] == count
            and params_here * 2 == count
            and planes == mesh.shape["slab"]
            and n * LANES == length == state.shape[2]
            and length % WIDE == 0
            and n == 2 * (WIDE // LANES)
        )
        local = functools.partial(pipelined, n) if fits else plain
        call = jax.shard_map(local, mesh=mesh, in_specs=in_specs, out_specs=out_specs, check_vma=False)
        return call(state, tangents, *others)

    return step
```

```python
import functools

import jax
import jax.numpy as jnp
from jax import lax
from jax.experimental import pallas as pl
from jax.experimental.pallas import tpu as pltpu
from jax.sharding import PartitionSpec as P


highest = lax.Precision.HIGHEST
time_step = 0.4
f32 = jnp.float32
bf16 = jnp.bfloat16
LANES = 128
WIDE = 2 * LANES
DEPTH = 32
PARTS = 1


def spread(values, fields):
    return values.reshape(values.shape + (1,) * (fields.ndim - values.ndim))


def reaction(state, tangent, coef, rates, offset):
    state_float = state.astype(f32)
    argument = jnp.einsum("ps,s...->p...", rates, state_float, precision=highest)
    activity = jnp.tanh(argument)
    slopes = 1.0 - activity * activity
    state_rate = jnp.einsum("ps,p...->s...", coef, activity, precision=highest)
    tangent_float = tangent.astype(f32)
    mixing = jnp.einsum("pt,qt...->qp...", rates, tangent_float, precision=highest)
    number = tangent.shape[0]
    own_coef = lax.dynamic_slice_in_dim(coef, offset, number, 0)
    own_activity = lax.dynamic_slice_in_dim(activity, offset, number, 0)
    tangent_rate = jnp.einsum("ps,qp...->qs...", coef, slopes[None] * mixing, precision=highest)
    tangent_rate = tangent_rate + spread(own_coef, tangent) * own_activity[:, None]
    return (state_rate, tangent_rate)


def update(fields, rate, speeds, diffusivity, operators):
    derivative_op, diffusion_op, filter_op = operators
    slope_term = jnp.dot(fields, derivative_op, preferred_element_type=f32)
    curve_term = jnp.dot(fields, diffusion_op, preferred_element_type=f32)
    middle = fields.astype(f32) + time_step * (
        spread(diffusivity, fields) * curve_term - spread(speeds, fields) * slope_term + rate
    )
    middle = middle.astype(bf16)
    return jnp.dot(middle, filter_op, preferred_element_type=f32).astype(bf16)


def plain(state, tangents, d1, d2, filt, advect, diffuse, coef, rates):
    params_here = tangents.shape[0]
    state_count = state.shape[0]
    offset = lax.axis_index("field") * params_here
    operators = (d1, d2, filt)
    for direction in range(2):
        speeds = advect[direction]
        state_rate, tangent_rate = reaction(state, tangents, coef, rates, offset)
        tangents = update(tangents, tangent_rate, speeds[None, :], diffuse[None, :], operators)
        outgoing = update(state, state_rate, speeds, diffuse, operators)
        merged = tangents.reshape((params_here * state_count,) + tangents.shape[2:])
        arrived = lax.all_to_all(outgoing, "pencil", split_axis=3, concat_axis=2, tiled=True)
        merged = lax.all_to_all(merged, "pencil", split_axis=3, concat_axis=2, tiled=True)
        state = jnp.swapaxes(arrived, 2, 3)
        merged = jnp.swapaxes(merged, 2, 3)
        tangents = merged.reshape((params_here, state_count) + merged.shape[1:])
    return (state, tangents)


def aligned(index, size):
    return pl.ds(pl.multiple_of(index * size, size), size)


def fill_mixer(entry, high, low):
    rows, columns = high.shape
    lane = lax.broadcasted_iota(jnp.int32, (8, columns), 1)
    row = lax.broadcasted_iota(jnp.int32, (8, columns), 0)
    group = lane // DEPTH
    within = lane - group * DEPTH
    for a in range(rows // DEPTH):
        values = jnp.zeros((8, columns), f32)
        for b in range(columns // DEPTH):
            values = jnp.where(group == b, entry(a, b), values)
        pieces = [jnp.where(within == row + 8 * k, values, 0.0) for k in range(DEPTH // 8)]
        block = jnp.concatenate(pieces, axis=0)
        rounded = block.astype(bf16)
        high[a * DEPTH : (a + 1) * DEPTH, :] = rounded
        low[a * DEPTH : (a + 1) * DEPTH, :] = (block - rounded.astype(f32)).astype(bf16)


def mixed(mixer, fields):
    high, low = mixer
    return jnp.dot(high[...], fields, preferred_element_type=f32) + jnp.dot(
        low[...], fields, preferred_element_type=f32
    )


def weighted(coef, s, channels):
    total = None
    for p in range(coef.shape[0]):
        term = coef[p, s] * channels[p * DEPTH : (p + 1) * DEPTH]
        total = term if total is None else total + term
    return total


def tangent_scaled(activity, mixing, own):
    scaled = (1.0 - activity * activity) * mixing
    group = lax.broadcasted_iota(jnp.int32, activity.shape, 0) // DEPTH
    return scaled + jnp.where(group == own, activity, 0.0)


def advance(v, curve, slope, rate, diffusivity, speed):
    return (v.astype(f32) + time_step * (diffusivity * curve - speed * slope + rate)).astype(bf16)


def x_state_kernel(n, part, *refs):
    kept = n // 2
    far, outs, near, rest = refs[:8], refs[8 : 9 + kept], refs[9 + kept : 17 + kept], refs[17 + kept :]
    rates, coef, advect, diffuse, state, d1, d2, filt = near
    filt_own, rates_high, rates_low, rate, middle, ready, sems, out_sems = rest
    me, half = lax.axis_index("pencil"), lax.axis_index("field")
    fields, _, rows, length = state.shape
    size = length // n
    sources = list(far)
    sources[4] = far[4].at[:, :, aligned(PARTS * half + part, rows), :]
    copies = [pltpu.make_async_copy(sources[i], near[i], sems.at[i]) for i in range(8)]
    for copy in copies:
        copy.start()
    for copy in copies[:4]:
        copy.wait()
    fill_mixer(lambda a, b: rates[a, b], rates_high, rates_low)
    for copy in copies[4:]:
        copy.wait()
    own = state[:, 0].reshape(fields * rows, length)
    for c in range(length // WIDE):
        across = slice(c * WIDE, (c + 1) * WIDE)
        for j in range(rows // DEPTH):
            u = state[:, 0, j * DEPTH : (j + 1) * DEPTH, across].reshape(fields * DEPTH, WIDE)
            activity = jnp.tanh(mixed((rates_high, rates_low), u))
            for s in range(fields):
                at = slice(s * rows + j * DEPTH, s * rows + (j + 1) * DEPTH)
                rate[at, across] = weighted(coef, s, activity)
        slope = jnp.dot(own, d1[:, across], preferred_element_type=f32)
        for s in range(fields):
            at = slice(s * rows, (s + 1) * rows)
            rate[at, across] = rate[at, across] - advect[0, s] * slope[at]
        curve = jnp.dot(own, d2[:, across], preferred_element_type=f32)
        for s in range(fields):
            at = slice(s * rows, (s + 1) * rows)
            moved = own[at, across].astype(f32) + time_step * (diffuse[s] * curve[at] + rate[at, across])
            middle[at, across] = moved.astype(bf16)
    for r in range(n):
        filt_own[:, r * size : (r + 1) * size] = filt[:, aligned(me ^ r, size)]
    for c in reversed(range(length // WIDE)):
        across = slice(c * WIDE, (c + 1) * WIDE)
        result = jnp.dot(middle[...], filt_own[:, across], preferred_element_type=f32).astype(bf16)
        for k in range(WIDE // size):
            r = c * (WIDE // size) + k
            ready[r] = result[:, k * size : (k + 1) * size].reshape(fields, rows, size)
        if c * (WIDE // size) == kept:
            sends = [pltpu.make_async_copy(ready.at[pl.ds(kept, n - kept)], outs[kept], out_sems.at[kept])]
            sends[0].start()
    for r in range(kept):
        sends.append(pltpu.make_async_copy(ready.at[r], outs[r], out_sems.at[r]))
        sends[-1].start()
    for send in sends:
        send.wait()


def x_kernel(n, q, params_here, rates, coef, advect, diffuse, state, tangent, d1, d2, filt, *rest):
    outs, rest = rest[:n], rest[n:]
    filt_own, rates_high, rates_low, middle = rest
    me, half = lax.axis_index("pencil"), lax.axis_index("field")
    count, rows, length = state.shape
    size = length // n

    @pl.when(pl.program_id(0) == 0)
    def _():
        fill_mixer(lambda a, b: rates[a, b], rates_high, rates_low)
        for r in range(n):
            filt_own[:, r * size : (r + 1) * size] = filt[:, aligned(me ^ r, size)]

    own = tangent[...].reshape(count * rows, length)
    for c in range(length // WIDE):
        across = slice(c * WIDE, (c + 1) * WIDE)
        u = state[:, :, across].reshape(count * rows, WIDE)
        activity = jnp.tanh(mixed((rates_high, rates_low), u))
        mixing = mixed((rates_high, rates_low), own[:, across])
        scaled = tangent_scaled(activity, mixing, half * params_here + q)
        slope = jnp.dot(own, d1[:, across], preferred_element_type=f32)
        curve = jnp.dot(own, d2[:, across], preferred_element_type=f32)
        for s in range(count):
            at = slice(s * rows, (s + 1) * rows)
            rate = weighted(coef, s, scaled)
            middle[at, across] = advance(
                own[at, across], curve[at], slope[at], rate, diffuse[s], advect[0, s]
            )
    result = jnp.dot(middle[...], filt_own[...], preferred_element_type=f32).astype(bf16)
    for r in range(n):
        outs[r][...] = result[:, r * size : (r + 1) * size].reshape(count, rows, size)


def y_kernel(n, q, params_here, rates, coef, advect, diffuse, *rest):
    pieces = PARTS * n
    own, other, rest = rest[:pieces], rest[pieces : 2 * pieces], rest[2 * pieces :]
    if q is not None:
        arrived, rest = rest[:n], rest[n:]
    d1t, d2t, filtt = rest[:3]
    outs, rest = rest[3 : 3 + n], rest[3 + n :]
    filt_own, u_full, rate_full, rates_high, rates_low = rest[:5]
    v_full = u_full if q is None else rest[5]
    me, half = lax.axis_index("pencil"), lax.axis_index("field")
    count, rows, size = own[0].shape
    fields = outs[0].shape[0]
    first = half * fields if q is None else 0
    fill_mixer(lambda a, b: rates[a, b], rates_high, rates_low)

    for r in range(n):
        filt_own[r * size : (r + 1) * size, :] = filtt[aligned(me ^ r, size), :]
        for s in range(count):
            across = slice(s * size, (s + 1) * size)
            for part in range(PARTS):
                here, there = PARTS * half + part, PARTS * (1 - half) + part
                u_full[aligned(2 * PARTS * (me ^ r) + here, rows), across] = own[part * n + r][s]
                u_full[aligned(2 * PARTS * (me ^ r) + there, rows), across] = other[part * n + r][s]
            if q is not None:
                v_full[aligned(me ^ r, size), across] = arrived[r][s]

    def pair(full, block):
        tiles = []
        for k in range(2):
            down = aligned(2 * block + k, DEPTH)
            tiles.append(
                jnp.concatenate([full[down, s * size : (s + 1) * size] for s in range(count)], axis=0)
            )
        return jnp.concatenate(tiles, axis=1)

    def rate_block(block, carry):
        scaled = jnp.tanh(mixed((rates_high, rates_low), pair(u_full, block)))
        if q is not None:
            mixing = mixed((rates_high, rates_low), pair(v_full, block))
            scaled = tangent_scaled(scaled, mixing, half * params_here + q)
        for s in range(fields):
            rate = weighted(coef, first + s, scaled)
            for k in range(2):
                rate_full[aligned(2 * block + k, DEPTH), s * size : (s + 1) * size] = rate[
                    :, k * size : (k + 1) * size
                ]
        return carry

    lax.fori_loop(0, n * size // (2 * DEPTH), rate_block, 0)

    def two_fields(f, carry):
        v = v_full[:, aligned(first // 2 + f, 2 * size)]
        slope = jnp.dot(d1t[...], v, preferred_element_type=f32)
        curve = jnp.dot(d2t[...], v, preferred_element_type=f32)
        columns = []
        for k in range(2):
            s = 2 * f + k
            across = slice(k * size, (k + 1) * size)
            columns.append(
                advance(
                    v[:, across],
                    curve[:, across],
                    slope[:, across],
                    rate_full[:, aligned(s, size)],
                    diffuse[first + s],
                    advect[1, first + s],
                )
            )
        middle = jnp.concatenate(columns, axis=1)
        result = jnp.dot(filt_own[...], middle, preferred_element_type=f32).astype(bf16)
        for r in range(n):
            for k in range(2):
                outs[r][2 * f + k] = result[r * size : (r + 1) * size, k * size : (k + 1) * size]
        return carry

    lax.fori_loop(0, fields // 2, two_fields, 0)


def place_kernel(n, q, some, *rest):
    out, sems = rest[-2:]
    me, half = lax.axis_index("pencil"), lax.axis_index("field")
    groups = 2 if q is None else 1
    copies = []
    for g in range(groups):
        for i, r in enumerate(some):
            slot = rest[g * n + i]
            here, _, size = slot.shape
            across = aligned(me ^ r, size)
            if q is None:
                target = out.at[aligned(half if g == 0 else 1 - half, here), 0, :, across]
            else:
                target = out.at[q, :, 0, :, across]
            copies.append(pltpu.make_async_copy(slot, target, sems.at[g * n + i]))
    for copy in copies:
        copy.start()
    for copy in copies:
        copy.wait()


SMEM = pl.BlockSpec(memory_space=pltpu.SMEM)
VMEM = pl.BlockSpec(memory_space=pltpu.VMEM)
HBM = pl.BlockSpec(memory_space=pl.ANY)
GRANT = pltpu.CompilerParams(vmem_limit_bytes=32 * 1024 * 1024)


def cost(flops, moved):
    return pl.CostEstimate(flops=flops, bytes_accessed=moved, transcendentals=0)


def mixers(fields, count):
    return [pltpu.VMEM((fields * DEPTH, count * DEPTH), bf16)] * 2


def x_state_call(n, part, scalars, state, d1, d2, filt):
    count, _, deep, length = state.shape
    rows = deep // (2 * PARTS)
    kept = n // 2
    block = (count, rows, length // n)
    square = pltpu.VMEM((length, length), bf16)
    return pl.pallas_call(
        functools.partial(x_state_kernel, n, part),
        out_shape=[jax.ShapeDtypeStruct(block, bf16)] * kept
        + [jax.ShapeDtypeStruct((n - kept,) + block, bf16)],
        in_specs=[HBM] * 8,
        out_specs=[HBM] * (kept + 1),
        scratch_shapes=[pltpu.SMEM(scalar.shape, f32) for scalar in scalars]
        + [pltpu.VMEM((count, 1, rows, length), bf16), square, square, square, square]
        + mixers(count, count)
        + [
            pltpu.VMEM((count * rows, length), f32),
            pltpu.VMEM((count * rows, length), bf16),
            pltpu.VMEM((n, count, rows, length // n), bf16),
            pltpu.SemaphoreType.DMA((8,)),
            pltpu.SemaphoreType.DMA((kept + 1,)),
        ],
        cost_estimate=cost(6 * count * rows * length * length, 4 * count * rows * length),
    )(*scalars, state, d1, d2, filt)


def x_call(n, q, scalars, state, tangents, d1, d2, filt):
    params_here, count, _, deep, length = tangents.shape
    size = length // n
    whole = pl.BlockSpec((length, length), lambda i: (0, 0))
    return pl.pallas_call(
        functools.partial(x_kernel, n, q, params_here),
        grid=(deep // DEPTH,),
        out_shape=[jax.ShapeDtypeStruct((count, deep, size), bf16)] * n,
        in_specs=[SMEM] * 4
        + [
            pl.BlockSpec((count, None, DEPTH, length), lambda i: (0, 0, i, 0)),
            pl.BlockSpec((None, count, None, DEPTH, length), lambda i: (q, 0, 0, i, 0)),
        ]
        + [whole] * 3,
        out_specs=[pl.BlockSpec((count, DEPTH, size), lambda i: (0, i, 0))] * n,
        scratch_shapes=[pltpu.VMEM((length, length), bf16)]
        + mixers(count, count)
        + [pltpu.VMEM((count * DEPTH, length), bf16)],
        cost_estimate=cost(6 * count * deep * length * length, 4 * count * deep * length),
    )(*scalars, state, tangents, d1, d2, filt)


def y_call(n, q, params_here, scalars, own, other, arrived, turned):
    count, _, size = own[0].shape
    length = size * n
    fields = count // 2 if q is None else count
    arrays = list(own) + list(other) + list(arrived or ())
    full = pltpu.VMEM((length, count * size), bf16)
    return pl.pallas_call(
        functools.partial(y_kernel, n, q, params_here),
        out_shape=[jax.ShapeDtypeStruct((fields, size, size), bf16)] * n,
        in_specs=[SMEM] * 4 + [VMEM] * (len(arrays) + 3),
        out_specs=[VMEM] * n,
        scratch_shapes=[pltpu.VMEM((length, length), bf16), full, pltpu.VMEM((length, fields * size), f32)]
        + mixers(count, count)
        + ([] if q is None else [full]),
        compiler_params=GRANT,
        cost_estimate=cost(6 * fields * size * length * length, 4 * fields * size * length),
    )(*scalars, *arrays, *turned)


def place_state(n, shape, own, other):
    return pl.pallas_call(
        functools.partial(place_kernel, n, None, range(n)),
        out_shape=jax.ShapeDtypeStruct(shape, bf16),
        in_specs=[VMEM] * (2 * n),
        out_specs=HBM,
        scratch_shapes=[pltpu.SemaphoreType.DMA((2 * n,))],
        compiler_params=GRANT,
        name="place_state",
    )(*own, *other)


def place_tangent(n, q, some, shape, slots, buffer):
    slots = [slots[r] for r in some]
    earlier = [] if buffer is None else [buffer]
    return pl.pallas_call(
        functools.partial(place_kernel, n, q, some),
        out_shape=jax.ShapeDtypeStruct(shape, bf16),
        in_specs=[VMEM] * len(slots) + [HBM] * len(earlier),
        out_specs=HBM,
        scratch_shapes=[pltpu.SemaphoreType.DMA((len(slots),))],
        input_output_aliases={len(slots): 0} if earlier else {},
        compiler_params=GRANT,
    )(*slots, *earlier)


def exchange(n, slots):
    order = list(range(n // 2, n)) + list(range(1, n // 2))
    arrived = {}
    for r in order:
        arrived[r] = lax.ppermute(slots[r], "pencil", [(i, i ^ r) for i in range(n)])
    return [slots[0]] + [arrived[r] for r in range(1, n)]


def exchange_state(n, made):
    kept = n // 2
    landed = lax.ppermute(made[kept], "pencil", [(i, i ^ (n - 1)) for i in range(n)])
    slots = list(made[:kept]) + [None] * (kept - 1) + [landed[kept - 1]]
    for r in range(1, kept):
        pairs = [(i, i ^ r) for i in range(n)]
        slots[r] = lax.ppermute(made[r], "pencil", pairs)
        slots[n - 1 - r] = lax.ppermute(landed[kept - 1 - r], "pencil", pairs)
    return slots


def swap(slots):
    return [lax.ppermute(slot, "field", [(0, 1), (1, 0)]) for slot in slots]


def pipelined(n, state, tangents, d1, d2, filt, advect, diffuse, coef, rates):
    params = range(tangents.shape[0])
    scalars = (rates, coef, advect, diffuse)

    def forth_state(part):
        return x_state_call(n, part, scalars, state, d1, d2, filt)

    def forth(q):
        return x_call(n, q, scalars, state, tangents, d1, d2, filt)

    own = []
    for part in range(PARTS):
        own += exchange_state(n, forth_state(part))
    sent = [exchange(n, forth(q)) for q in params]
    turned = (d1.T, d2.T, filt.T)
    other = swap(own)

    def turn(q):
        return y_call(n, q, len(params), scalars, own, other, None if q is None else sent[q], turned)

    mine = exchange(n, turn(None))
    theirs = swap(mine)
    buffer = None
    for q in params:
        back = exchange(n, turn(q))
        early = range(n if q < params[-1] else n - 1)
        buffer = place_tangent(n, q, early, tangents.shape, back, buffer)
    buffer = place_tangent(n, q, range(n - 1, n), tangents.shape, back, buffer)
    return (place_state(n, state.shape, mine, theirs), buffer)


def solution(mesh):
    in_specs = (
        P("parts", "slab", "pencil", None),
        P(("parts", "field"), None, "slab", "pencil", None),
        P(),
        P(),
        P(),
        P(),
        P(),
        P(),
        P(),
    )
    out_specs = (
        P("parts", "slab", "pencil", None),
        P(("parts", "field"), None, "slab", "pencil", None),
    )
    n = mesh.shape["pencil"]

    def step(state, tangents, *others):
        count, planes, _, length = state.shape
        count //= mesh.shape["parts"]
        params_here = tangents.shape[0] // (mesh.shape["parts"] * mesh.shape["field"])
        fits = (
            n & (n - 1) == 0
            and mesh.shape["field"] == 2
            and count * DEPTH == WIDE
            and others[-1].shape[0] == count
            and params_here * 2 == count
            and planes == mesh.shape["slab"]
            and n * LANES == length == state.shape[2]
            and length % WIDE == 0
            and n == 2 * (WIDE // LANES)
        )
        local = functools.partial(pipelined, n) if fits else plain
        call = jax.shard_map(local, mesh=mesh, in_specs=in_specs, out_specs=out_specs, check_vma=False)
        return call(state, tangents, *others)

    return step
```

```python
import functools

import jax
import jax.numpy as jnp
from jax import lax
from jax.experimental import pallas as pl
from jax.experimental.pallas import tpu as pltpu
from jax.sharding import PartitionSpec as P


highest = lax.Precision.HIGHEST
time_step = 0.4
f32 = jnp.float32
bf16 = jnp.bfloat16
LANES = 128
WIDE = 2 * LANES
DEPTH = 32
PARTS = 1


def spread(values, fields):
    return values.reshape(values.shape + (1,) * (fields.ndim - values.ndim))


def reaction(state, tangent, coef, rates, offset):
    state_float = state.astype(f32)
    argument = jnp.einsum("ps,s...->p...", rates, state_float, precision=highest)
    activity = jnp.tanh(argument)
    slopes = 1.0 - activity * activity
    state_rate = jnp.einsum("ps,p...->s...", coef, activity, precision=highest)
    tangent_float = tangent.astype(f32)
    mixing = jnp.einsum("pt,qt...->qp...", rates, tangent_float, precision=highest)
    number = tangent.shape[0]
    own_coef = lax.dynamic_slice_in_dim(coef, offset, number, 0)
    own_activity = lax.dynamic_slice_in_dim(activity, offset, number, 0)
    tangent_rate = jnp.einsum("ps,qp...->qs...", coef, slopes[None] * mixing, precision=highest)
    tangent_rate = tangent_rate + spread(own_coef, tangent) * own_activity[:, None]
    return (state_rate, tangent_rate)


def update(fields, rate, speeds, diffusivity, operators):
    derivative_op, diffusion_op, filter_op = operators
    slope_term = jnp.dot(fields, derivative_op, preferred_element_type=f32)
    curve_term = jnp.dot(fields, diffusion_op, preferred_element_type=f32)
    middle = fields.astype(f32) + time_step * (
        spread(diffusivity, fields) * curve_term - spread(speeds, fields) * slope_term + rate
    )
    middle = middle.astype(bf16)
    return jnp.dot(middle, filter_op, preferred_element_type=f32).astype(bf16)


def plain(state, tangents, d1, d2, filt, advect, diffuse, coef, rates):
    params_here = tangents.shape[0]
    state_count = state.shape[0]
    offset = lax.axis_index("field") * params_here
    operators = (d1, d2, filt)
    for direction in range(2):
        speeds = advect[direction]
        state_rate, tangent_rate = reaction(state, tangents, coef, rates, offset)
        tangents = update(tangents, tangent_rate, speeds[None, :], diffuse[None, :], operators)
        outgoing = update(state, state_rate, speeds, diffuse, operators)
        merged = tangents.reshape((params_here * state_count,) + tangents.shape[2:])
        arrived = lax.all_to_all(outgoing, "pencil", split_axis=3, concat_axis=2, tiled=True)
        merged = lax.all_to_all(merged, "pencil", split_axis=3, concat_axis=2, tiled=True)
        state = jnp.swapaxes(arrived, 2, 3)
        merged = jnp.swapaxes(merged, 2, 3)
        tangents = merged.reshape((params_here, state_count) + merged.shape[1:])
    return (state, tangents)


def aligned(index, size):
    return pl.ds(pl.multiple_of(index * size, size), size)


def fill_mixer(entry, high, low):
    rows, columns = high.shape
    lane = lax.broadcasted_iota(jnp.int32, (8, columns), 1)
    row = lax.broadcasted_iota(jnp.int32, (8, columns), 0)
    group = lane // DEPTH
    within = lane - group * DEPTH
    for a in range(rows // DEPTH):
        values = jnp.zeros((8, columns), f32)
        for b in range(columns // DEPTH):
            values = jnp.where(group == b, entry(a, b), values)
        pieces = [jnp.where(within == row + 8 * k, values, 0.0) for k in range(DEPTH // 8)]
        block = jnp.concatenate(pieces, axis=0)
        rounded = block.astype(bf16)
        high[a * DEPTH : (a + 1) * DEPTH, :] = rounded
        low[a * DEPTH : (a + 1) * DEPTH, :] = (block - rounded.astype(f32)).astype(bf16)


def mixed(mixer, fields):
    high, low = mixer
    return jnp.dot(high[...], fields, preferred_element_type=f32) + jnp.dot(
        low[...], fields, preferred_element_type=f32
    )


def weighted(coef, s, channels):
    total = None
    for p in range(coef.shape[0]):
        term = coef[p, s] * channels[p * DEPTH : (p + 1) * DEPTH]
        total = term if total is None else total + term
    return total


def tangent_scaled(activity, mixing, own):
    scaled = (1.0 - activity * activity) * mixing
    group = lax.broadcasted_iota(jnp.int32, activity.shape, 0) // DEPTH
    return scaled + jnp.where(group == own, activity, 0.0)


def advance(v, curve, slope, rate, diffusivity, speed):
    return (v.astype(f32) + time_step * (diffusivity * curve - speed * slope + rate)).astype(bf16)


def x_state_kernel(n, part, *refs):
    kept = n // 2
    far, outs, near, rest = refs[:8], refs[8 : 9 + kept], refs[9 + kept : 17 + kept], refs[17 + kept :]
    rates, coef, advect, diffuse, state, d1, d2, filt = near
    filt_own, rates_high, rates_low, rate, middle, ready, sems, out_sems = rest
    me, half = lax.axis_index("pencil"), lax.axis_index("field")
    fields, _, rows, length = state.shape
    size = length // n
    sources = list(far)
    sources[4] = far[4].at[:, :, aligned(PARTS * half + part, rows), :]
    copies = [pltpu.make_async_copy(sources[i], near[i], sems.at[i]) for i in range(8)]
    for i in (0, 4, 5, 6, 7, 1, 2, 3):
        copies[i].start()
    copies[0].wait()
    fill_mixer(lambda a, b: rates[a, b], rates_high, rates_low)
    for copy in copies[1:]:
        copy.wait()
    own = state[:, 0].reshape(fields * rows, length)
    for c in range(length // WIDE):
        across = slice(c * WIDE, (c + 1) * WIDE)
        for j in range(rows // DEPTH):
            u = state[:, 0, j * DEPTH : (j + 1) * DEPTH, across].reshape(fields * DEPTH, WIDE)
            activity = jnp.tanh(mixed((rates_high, rates_low), u))
            for s in range(fields):
                at = slice(s * rows + j * DEPTH, s * rows + (j + 1) * DEPTH)
                rate[at, across] = weighted(coef, s, activity)
        slope = jnp.dot(own, d1[:, across], preferred_element_type=f32)
        for s in range(fields):
            at = slice(s * rows, (s + 1) * rows)
            rate[at, across] = rate[at, across] - advect[0, s] * slope[at]
        curve = jnp.dot(own, d2[:, across], preferred_element_type=f32)
        for s in range(fields):
            at = slice(s * rows, (s + 1) * rows)
            moved = own[at, across].astype(f32) + time_step * (diffuse[s] * curve[at] + rate[at, across])
            middle[at, across] = moved.astype(bf16)
    for r in range(n):
        filt_own[:, r * size : (r + 1) * size] = filt[:, aligned(me ^ r, size)]
    for c in reversed(range(length // WIDE)):
        across = slice(c * WIDE, (c + 1) * WIDE)
        result = jnp.dot(middle[...], filt_own[:, across], preferred_element_type=f32).astype(bf16)
        for k in range(WIDE // size):
            r = c * (WIDE // size) + k
            ready[r] = result[:, k * size : (k + 1) * size].reshape(fields, rows, size)
        if c * (WIDE // size) == kept:
            sends = [pltpu.make_async_copy(ready.at[pl.ds(kept, n - kept)], outs[kept], out_sems.at[kept])]
            sends[0].start()
    for r in range(kept):
        sends.append(pltpu.make_async_copy(ready.at[r], outs[r], out_sems.at[r]))
        sends[-1].start()
    for send in sends:
        send.wait()


def x_kernel(n, q, params_here, rates, coef, advect, diffuse, state, tangent, d1, d2, filt, *rest):
    outs, rest = rest[:n], rest[n:]
    filt_own, rates_high, rates_low, middle = rest
    me, half = lax.axis_index("pencil"), lax.axis_index("field")
    count, rows, length = state.shape
    size = length // n

    @pl.when(pl.program_id(0) == 0)
    def _():
        fill_mixer(lambda a, b: rates[a, b], rates_high, rates_low)
        for r in range(n):
            filt_own[:, r * size : (r + 1) * size] = filt[:, aligned(me ^ r, size)]

    own = tangent[...].reshape(count * rows, length)
    for c in range(length // WIDE):
        across = slice(c * WIDE, (c + 1) * WIDE)
        u = state[:, :, across].reshape(count * rows, WIDE)
        activity = jnp.tanh(mixed((rates_high, rates_low), u))
        mixing = mixed((rates_high, rates_low), own[:, across])
        scaled = tangent_scaled(activity, mixing, half * params_here + q)
        slope = jnp.dot(own, d1[:, across], preferred_element_type=f32)
        curve = jnp.dot(own, d2[:, across], preferred_element_type=f32)
        for s in range(count):
            at = slice(s * rows, (s + 1) * rows)
            rate = weighted(coef, s, scaled)
            middle[at, across] = advance(
                own[at, across], curve[at], slope[at], rate, diffuse[s], advect[0, s]
            )
    result = jnp.dot(middle[...], filt_own[...], preferred_element_type=f32).astype(bf16)
    for r in range(n):
        outs[r][...] = result[:, r * size : (r + 1) * size].reshape(count, rows, size)


def y_kernel(n, q, params_here, rates, coef, advect, diffuse, *rest):
    pieces = PARTS * n
    own, other, rest = rest[:pieces], rest[pieces : 2 * pieces], rest[2 * pieces :]
    if q is not None:
        arrived, rest = rest[:n], rest[n:]
    d1t, d2t, filtt = rest[:3]
    outs, rest = rest[3 : 3 + n], rest[3 + n :]
    filt_own, u_full, rate_full, rates_high, rates_low = rest[:5]
    v_full = u_full if q is None else rest[5]
    me, half = lax.axis_index("pencil"), lax.axis_index("field")
    count, rows, size = own[0].shape
    fields = outs[0].shape[0]
    first = half * fields if q is None else 0
    fill_mixer(lambda a, b: rates[a, b], rates_high, rates_low)

    for r in range(n):
        filt_own[r * size : (r + 1) * size, :] = filtt[aligned(me ^ r, size), :]
        for s in range(count):
            across = slice(s * size, (s + 1) * size)
            for part in range(PARTS):
                here, there = PARTS * half + part, PARTS * (1 - half) + part
                u_full[aligned(2 * PARTS * (me ^ r) + here, rows), across] = own[part * n + r][s]
                u_full[aligned(2 * PARTS * (me ^ r) + there, rows), across] = other[part * n + r][s]
            if q is not None:
                v_full[aligned(me ^ r, size), across] = arrived[r][s]

    def pair(full, block):
        tiles = []
        for k in range(2):
            down = aligned(2 * block + k, DEPTH)
            tiles.append(
                jnp.concatenate([full[down, s * size : (s + 1) * size] for s in range(count)], axis=0)
            )
        return jnp.concatenate(tiles, axis=1)

    def rate_block(block, carry):
        scaled = jnp.tanh(mixed((rates_high, rates_low), pair(u_full, block)))
        if q is not None:
            mixing = mixed((rates_high, rates_low), pair(v_full, block))
            scaled = tangent_scaled(scaled, mixing, half * params_here + q)
        for s in range(fields):
            rate = weighted(coef, first + s, scaled)
            for k in range(2):
                rate_full[aligned(2 * block + k, DEPTH), s * size : (s + 1) * size] = rate[
                    :, k * size : (k + 1) * size
                ]
        return carry

    lax.fori_loop(0, n * size // (2 * DEPTH), rate_block, 0)

    def two_fields(f, carry):
        v = v_full[:, aligned(first // 2 + f, 2 * size)]
        slope = jnp.dot(d1t[...], v, preferred_element_type=f32)
        curve = jnp.dot(d2t[...], v, preferred_element_type=f32)
        columns = []
        for k in range(2):
            s = 2 * f + k
            across = slice(k * size, (k + 1) * size)
            columns.append(
                advance(
                    v[:, across],
                    curve[:, across],
                    slope[:, across],
                    rate_full[:, aligned(s, size)],
                    diffuse[first + s],
                    advect[1, first + s],
                )
            )
        middle = jnp.concatenate(columns, axis=1)
        result = jnp.dot(filt_own[...], middle, preferred_element_type=f32).astype(bf16)
        for r in range(n):
            for k in range(2):
                outs[r][2 * f + k] = result[r * size : (r + 1) * size, k * size : (k + 1) * size]
        return carry

    lax.fori_loop(0, fields // 2, two_fields, 0)


def place_kernel(n, q, some, *rest):
    out, sems = rest[-2:]
    me, half = lax.axis_index("pencil"), lax.axis_index("field")
    groups = 2 if q is None else 1
    copies = []
    for g in range(groups):
        for i, r in enumerate(some):
            slot = rest[g * n + i]
            here, _, size = slot.shape
            across = aligned(me ^ r, size)
            if q is None:
                target = out.at[aligned(half if g == 0 else 1 - half, here), 0, :, across]
            else:
                target = out.at[q, :, 0, :, across]
            copies.append(pltpu.make_async_copy(slot, target, sems.at[g * n + i]))
    for copy in copies:
        copy.start()
    for copy in copies:
        copy.wait()


SMEM = pl.BlockSpec(memory_space=pltpu.SMEM)
VMEM = pl.BlockSpec(memory_space=pltpu.VMEM)
HBM = pl.BlockSpec(memory_space=pl.ANY)
GRANT = pltpu.CompilerParams(vmem_limit_bytes=32 * 1024 * 1024)


def cost(flops, moved):
    return pl.CostEstimate(flops=flops, bytes_accessed=moved, transcendentals=0)


def mixers(fields, count):
    return [pltpu.VMEM((fields * DEPTH, count * DEPTH), bf16)] * 2


def x_state_call(n, part, scalars, state, d1, d2, filt):
    count, _, deep, length = state.shape
    rows = deep // (2 * PARTS)
    kept = n // 2
    block = (count, rows, length // n)
    square = pltpu.VMEM((length, length), bf16)
    return pl.pallas_call(
        functools.partial(x_state_kernel, n, part),
        out_shape=[jax.ShapeDtypeStruct(block, bf16)] * kept
        + [jax.ShapeDtypeStruct((n - kept,) + block, bf16)],
        in_specs=[HBM] * 8,
        out_specs=[HBM] * (kept + 1),
        scratch_shapes=[pltpu.SMEM(scalar.shape, f32) for scalar in scalars]
        + [pltpu.VMEM((count, 1, rows, length), bf16), square, square, square, square]
        + mixers(count, count)
        + [
            pltpu.VMEM((count * rows, length), f32),
            pltpu.VMEM((count * rows, length), bf16),
            pltpu.VMEM((n, count, rows, length // n), bf16),
            pltpu.SemaphoreType.DMA((8,)),
            pltpu.SemaphoreType.DMA((kept + 1,)),
        ],
        cost_estimate=cost(6 * count * rows * length * length, 4 * count * rows * length),
    )(*scalars, state, d1, d2, filt)


def x_call(n, q, scalars, state, tangents, d1, d2, filt):
    params_here, count, _, deep, length = tangents.shape
    size = length // n
    whole = pl.BlockSpec((length, length), lambda i: (0, 0))
    return pl.pallas_call(
        functools.partial(x_kernel, n, q, params_here),
        grid=(deep // DEPTH,),
        out_shape=[jax.ShapeDtypeStruct((count, deep, size), bf16)] * n,
        in_specs=[SMEM] * 4
        + [
            pl.BlockSpec((count, None, DEPTH, length), lambda i: (0, 0, i, 0)),
            pl.BlockSpec((None, count, None, DEPTH, length), lambda i: (q, 0, 0, i, 0)),
        ]
        + [whole] * 3,
        out_specs=[pl.BlockSpec((count, DEPTH, size), lambda i: (0, i, 0))] * n,
        scratch_shapes=[pltpu.VMEM((length, length), bf16)]
        + mixers(count, count)
        + [pltpu.VMEM((count * DEPTH, length), bf16)],
        cost_estimate=cost(6 * count * deep * length * length, 4 * count * deep * length),
    )(*scalars, state, tangents, d1, d2, filt)


def y_call(n, q, params_here, scalars, own, other, arrived, turned):
    count, _, size = own[0].shape
    length = size * n
    fields = count // 2 if q is None else count
    arrays = list(own) + list(other) + list(arrived or ())
    full = pltpu.VMEM((length, count * size), bf16)
    return pl.pallas_call(
        functools.partial(y_kernel, n, q, params_here),
        out_shape=[jax.ShapeDtypeStruct((fields, size, size), bf16)] * n,
        in_specs=[SMEM] * 4 + [VMEM] * (len(arrays) + 3),
        out_specs=[VMEM] * n,
        scratch_shapes=[pltpu.VMEM((length, length), bf16), full, pltpu.VMEM((length, fields * size), f32)]
        + mixers(count, count)
        + ([] if q is None else [full]),
        compiler_params=GRANT,
        cost_estimate=cost(6 * fields * size * length * length, 4 * fields * size * length),
    )(*scalars, *arrays, *turned)


def place_state(n, shape, own, other):
    return pl.pallas_call(
        functools.partial(place_kernel, n, None, range(n)),
        out_shape=jax.ShapeDtypeStruct(shape, bf16),
        in_specs=[VMEM] * (2 * n),
        out_specs=HBM,
        scratch_shapes=[pltpu.SemaphoreType.DMA((2 * n,))],
        compiler_params=GRANT,
        name="place_state",
    )(*own, *other)


def place_tangent(n, q, some, shape, slots, buffer):
    slots = [slots[r] for r in some]
    earlier = [] if buffer is None else [buffer]
    return pl.pallas_call(
        functools.partial(place_kernel, n, q, some),
        out_shape=jax.ShapeDtypeStruct(shape, bf16),
        in_specs=[VMEM] * len(slots) + [HBM] * len(earlier),
        out_specs=HBM,
        scratch_shapes=[pltpu.SemaphoreType.DMA((len(slots),))],
        input_output_aliases={len(slots): 0} if earlier else {},
        compiler_params=GRANT,
    )(*slots, *earlier)


def exchange(n, slots):
    order = list(range(n // 2, n)) + list(range(1, n // 2))
    arrived = {}
    for r in order:
        arrived[r] = lax.ppermute(slots[r], "pencil", [(i, i ^ r) for i in range(n)])
    return [slots[0]] + [arrived[r] for r in range(1, n)]


def exchange_state(n, made):
    kept = n // 2
    landed = lax.ppermute(made[kept], "pencil", [(i, i ^ (n - 1)) for i in range(n)])
    slots = list(made[:kept]) + [None] * (kept - 1) + [landed[kept - 1]]
    for r in range(1, kept):
        pairs = [(i, i ^ r) for i in range(n)]
        slots[r] = lax.ppermute(made[r], "pencil", pairs)
        slots[n - 1 - r] = lax.ppermute(landed[kept - 1 - r], "pencil", pairs)
    return slots


def swap(slots):
    return [lax.ppermute(slot, "field", [(0, 1), (1, 0)]) for slot in slots]


def pipelined(n, state, tangents, d1, d2, filt, advect, diffuse, coef, rates):
    params = range(tangents.shape[0])
    scalars = (rates, coef, advect, diffuse)

    def forth_state(part):
        return x_state_call(n, part, scalars, state, d1, d2, filt)

    def forth(q):
        return x_call(n, q, scalars, state, tangents, d1, d2, filt)

    own = []
    for part in range(PARTS):
        own += exchange_state(n, forth_state(part))
    sent = [exchange(n, forth(q)) for q in params]
    turned = (d1.T, d2.T, filt.T)
    other = swap(own)

    def turn(q):
        return y_call(n, q, len(params), scalars, own, other, None if q is None else sent[q], turned)

    mine = exchange(n, turn(None))
    theirs = swap(mine)
    buffer = None
    for q in params:
        back = exchange(n, turn(q))
        early = range(n if q < params[-1] else n - 1)
        buffer = place_tangent(n, q, early, tangents.shape, back, buffer)
    buffer = place_tangent(n, q, range(n - 1, n), tangents.shape, back, buffer)
    return (place_state(n, state.shape, mine, theirs), buffer)


def solution(mesh):
    in_specs = (
        P("parts", "slab", "pencil", None),
        P(("parts", "field"), None, "slab", "pencil", None),
        P(),
        P(),
        P(),
        P(),
        P(),
        P(),
        P(),
    )
    out_specs = (
        P("parts", "slab", "pencil", None),
        P(("parts", "field"), None, "slab", "pencil", None),
    )
    n = mesh.shape["pencil"]

    def step(state, tangents, *others):
        count, planes, _, length = state.shape
        count //= mesh.shape["parts"]
        params_here = tangents.shape[0] // (mesh.shape["parts"] * mesh.shape["field"])
        fits = (
            n & (n - 1) == 0
            and mesh.shape["field"] == 2
            and count * DEPTH == WIDE
            and others[-1].shape[0] == count
            and params_here * 2 == count
            and planes == mesh.shape["slab"]
            and n * LANES == length == state.shape[2]
            and length % WIDE == 0
            and n == 2 * (WIDE // LANES)
        )
        local = functools.partial(pipelined, n) if fits else plain
        call = jax.shard_map(local, mesh=mesh, in_specs=in_specs, out_specs=out_specs, check_vma=False)
        return call(state, tangents, *others)

    return step
```
